128 devices in a mesh: seq: 64 (over x_lo, z, y, core), ch: 2 (over x_hi).
Axes of the slice: x: 4 (x_hi: 2, x_lo: 2; x = x_hi * 2 + x_lo), y: 4, z: 4, core: 2. Of those that a mesh axis runs over, the one named last changes fastest.
Arguments:
- inputs: bfloat16 [4, 16384, 1536], P(None, 'seq', 'ch'), may hold values from -6 to 6
- kernels: float32 [3, 3, 1536], P(None, None, 'ch'), may hold values from -3.5 to 3.5
- mixers: bfloat16 [3, 1536, 1536], P(None, None, 'ch'), may hold values from -0.15625 to 0.15625
- cotangent: bfloat16 [4, 16384, 1536], P(None, 'seq', 'ch'), may hold values from -6 to 6
Outputs:
- outputs: bfloat16 [4, 16384, 1536], P(None, 'seq', 'ch')
- input_grad: bfloat16 [4, 16384, 1536], P(None, 'seq', 'ch')
- mixer_grads: float32 [3, 1536, 1536], P(None, 'seq', 'ch')
The draws below stay inside these ranges and needn't reach their ends.
All inputs are finite; a program needn't handle non-finite values.
Results may differ from the reference program's by a relative error of at most 0.0075.
Values may be sent and summed in bfloat16 or wider, within the bound.
A program may use at most 128 MiB of HBM per device.

```python
import math
import jax
import jax.numpy as jnp

C = 1536
SEQS = 4
BLOCKS = 3
BINS = 16384


def levels(key, dims, shards, low, high):
    factor_of, own = 1.0, jax.random.fold_in(key, 6)
    for axis_at, blocks in shards:
        steps = jnp.exp(jax.random.uniform(jax.random.fold_in(own, axis_at), (blocks,), jnp.float32, low / len(shards), high / len(shards)))
        factor_of = factor_of * jnp.repeat(steps, dims[axis_at] // blocks).reshape([-1 if axis == axis_at else 1 for axis in range(len(dims))])
    return factor_of


def gaussian(stream_key, dims, scale, limit, cuts=(), dtype=jnp.bfloat16):
    factor_of = levels(stream_key, dims, cuts, -0.22, 0.18) if cuts else 1.0
    values = jax.random.normal(stream_key, dims, jnp.float32) * scale * factor_of
    return jnp.minimum(jnp.maximum(values, -limit), limit).astype(dtype)


def setup_inputs(seed: int = 0) -> dict:
    splits = jax.random.split(jax.random.key(seed), 5)
    return {
        "inputs": gaussian(splits[0], (SEQS, BINS, C), 1.0, 6.0, ((1, 64), (2, 2))),
        "kernels": gaussian(splits[1], (BLOCKS, 3, C), 3 ** -0.5, 3.5, ((2, 2),), jnp.float32),
        "mixers": gaussian(splits[2], (BLOCKS, C, C), C ** -0.5, 0.15625, ((2, 2),)),
        "cotangent": gaussian(splits[3], (SEQS, BINS, C), 1.0, 6.0, ((1, 64), (2, 2))),
    }


dilations = (2, 4, 8)

def gelu_exact(value):
    return 0.5 * value * (1.0 + jax.scipy.special.erf(value * 0.7071067811865476))

def gelu_slope(value):
    return 0.5 * (1.0 + jax.scipy.special.erf(value * 0.7071067811865476)) + value * jnp.exp(-0.5 * value * value) * 0.3989422804014327

def reference(inputs, kernels, mixers, cotangent):
    seqs, bins, chans = inputs.shape
    current = inputs
    saved = []
    for block, width in enumerate(dilations):
        padded = jnp.pad(current.astype(jnp.float32), ((0, 0), (width, width), (0, 0)))
        pre = kernels[block, 0] * padded[:, 0:bins] + kernels[block, 1] * padded[:, width:width + bins] + kernels[block, 2] * padded[:, 2 * width:2 * width + bins]
        act = gelu_exact(pre).astype(jnp.bfloat16)
        mixed = jnp.dot(act.reshape(-1, chans), mixers[block], preferred_element_type=jnp.float32)
        current = (current.astype(jnp.float32) + mixed.reshape(seqs, bins, chans)).astype(jnp.bfloat16)
        saved.append((pre, act))
    scale = 1.0 / math.sqrt(seqs * bins)
    grad_list = [None, None, None]
    upper = cotangent
    for block in (2, 1, 0):
        width = dilations[block]
        pre, act = saved[block]
        flat = upper.reshape(-1, chans)
        back = jnp.dot(flat, mixers[block].T, preferred_element_type=jnp.float32).reshape(seqs, bins, chans)
        slope = (back * gelu_slope(pre)).astype(jnp.bfloat16)
        grad_list[block] = jnp.dot(act.reshape(-1, chans).T, flat, preferred_element_type=jnp.float32) * scale
        padded = jnp.pad(slope.astype(jnp.float32), ((0, 0), (width, width), (0, 0)))
        lower = upper.astype(jnp.float32) + kernels[block, 0] * padded[:, 2 * width:2 * width + bins] + kernels[block, 1] * padded[:, width:width + bins] + kernels[block, 2] * padded[:, 0:bins]
        upper = lower.astype(jnp.bfloat16)
    return (current, upper, jnp.stack(grad_list))
```

```python
import jax
import jax.numpy as jnp
from jax import lax
from jax.experimental import pallas as pl
from jax.experimental.pallas import tpu as pltpu
from jax.sharding import PartitionSpec as P

dilations = (2, 4, 8)
MESH = pl.DeviceIdType.MESH
ANY = pl.BlockSpec(memory_space=pl.ANY)
bf16, f32 = jnp.bfloat16, jnp.float32
XH, EH = 32, 16
BINS, HALF, FULL = 256, 768, 1536


def place():
    s = lax.axis_index("seq")
    h = lax.axis_index("ch")
    core = lax.rem(s, 2)
    y = lax.rem(s // 2, 4)
    z = lax.rem(s // 8, 4)
    return s, h, s // 32, z, y, core


def other(s):
    return lax.rem(s + 32, 64)


def line(core, low, a, b):
    z = a + core * (b - a)
    y = b + core * (a - b)
    return low * 32 + z * 8 + y * 2 + core


def remote(src, dst, send, recv, to):
    return pltpu.make_async_remote_copy(
        src_ref=src, dst_ref=dst, send_sem=send, recv_sem=recv, device_id=to, device_id_type=MESH
    )


def in_kernel(x_ref, e_ref, m_ref, k_ref, xo, eo, mo, ko, xs, xr, ms, mr, ls):
    s, h, low, z, y, core = place()
    g = other(s)
    cols = pl.ds(pl.multiple_of(h * HALF, HALF), HALF)
    opp = pl.ds(pl.multiple_of((1 - h) * HALF, HALF), HALF)
    a = z + core * (y - z)
    b = y + core * (z - y)
    piece = core * 16 + a * 4 + b

    def rows(first, count):
        return pl.ds(pl.multiple_of(first * 48, 48), count * 48)

    mine = m_ref.at[:, rows(piece, 1), :]
    first = remote(mine, mo.at[:, rows(piece, 1), cols], ms.at[0], mr.at[0], (g, 1 - h))
    first.start()
    kcopy = remote(k_ref, ko.at[h], ms.at[1], mr.at[1], (g, 1 - h))
    kcopy.start()

    sends = []
    for t, (src, dst, halo) in enumerate(((x_ref, xo, XH), (e_ref, eo, EH))):
        for p in range(2):
            pair = pl.ds(2 * p, 2)
            sends.append((None, remote(src.at[pair], dst.at[:, halo : halo + BINS, cols], xs.at[t, p, 0], xr.at[t, h, 0], (g, p))))
            sends.append((s < 63, remote(
                src.at[pair, BINS - halo : BINS], dst.at[:, 0:halo, cols], xs.at[t, p, 1], xr.at[t, h, 1], (other(lax.rem(s + 1, 64)), p))))
            sends.append((s > 0, remote(
                src.at[pair, 0:halo], dst.at[:, halo + BINS : 2 * halo + BINS, cols], xs.at[t, p, 2], xr.at[t, h, 2], (other(lax.rem(s + 63, 64)), p))))
    for cond, copy in sends:
        if cond is None:
            copy.start()
        else:
            pl.when(cond)(copy.start)
    local = pltpu.make_async_copy(m_ref, mo.at[:, :, cols], ls.at[0])
    local.start()
    klocal = pltpu.make_async_copy(k_ref, ko.at[h], ls.at[1])
    klocal.start()

    def spread(step, count, start, peer):
        copies = []
        for k in (1, 3, 2):
            copies.append(remote(
                mo.at[:, rows(start, count), opp], mo.at[:, rows(start, count), opp], ms.at[2 + step * 3 + k - 1], mr.at[2 + step * 3 + k - 1], peer(k)))
        for copy in copies:
            copy.start()
        for copy in copies:
            copy.wait_recv()
        return copies

    remote(mine, mo.at[:, rows(piece, 1), opp], ms.at[0], mr.at[0], (g, 1 - h)).wait_recv()
    step1 = spread(0, 1, piece, lambda k: (line(core, low, a, lax.rem(b + k, 4)), h))
    step2 = spread(1, 4, core * 16 + a * 4, lambda k: (line(core, low, lax.rem(a + k, 4), b), h))
    last = remote(mo.at[:, rows(core * 16, 16), opp], mo.at[:, rows(core * 16, 16), opp], ms.at[8], mr.at[8], (s + 1 - 2 * core, h))
    last.start()
    last.wait_recv()

    for t, (src, dst, halo) in enumerate(((x_ref, xo, XH), (e_ref, eo, EH))):
        for c in range(2):
            half = pl.ds(c * HALF, HALF)
            remote(src.at[0:2], dst.at[:, halo : halo + BINS, half], xs.at[t, 0, 0], xr.at[t, c, 0], (g, 0)).wait_recv()
            pl.when(g > 0)(remote(src.at[0:2, 0:halo], dst.at[:, 0:halo, half], xs.at[t, 0, 1], xr.at[t, c, 1], (g, 0)).wait_recv)
            pl.when(g < 63)(remote(src.at[0:2, 0:halo], dst.at[:, 0:halo, half], xs.at[t, 0, 2], xr.at[t, c, 2], (g, 0)).wait_recv)
    kcopy.wait_recv()
    local.wait()
    klocal.wait()
    for cond, copy in sends:
        if cond is None:
            copy.wait_send()
        else:
            pl.when(cond)(copy.wait_send)
    for copy in [first, kcopy, last, *step1, *step2]:
        copy.wait_send()


def gather(x, e, m, k):
    D = pltpu.SemaphoreType.DMA
    return pl.pallas_call(
        in_kernel,
        out_shape=(
            jax.ShapeDtypeStruct((2, BINS + 2 * XH, FULL), bf16),
            jax.ShapeDtypeStruct((2, BINS + 2 * EH, FULL), bf16),
            jax.ShapeDtypeStruct((3, FULL, FULL), bf16),
            jax.ShapeDtypeStruct((2, 9, HALF), f32),
        ),
        in_specs=[ANY] * 4,
        out_specs=(ANY,) * 4,
        scratch_shapes=[D((2, 2, 3)), D((2, 2, 3)), D((9,)), D((9,)), D((2,))],
        compiler_params=pltpu.CompilerParams(has_side_effects=True),
    )(x, e, m, k)


def out_kernel(x_ref, e_ref, g_ref, xo, eo, mg, own, got, part, t1, u1, mid, t2, u2, end, v3, fin, swap, rs, rr, ss, sr, ls):
    s, h, low, z, y, core = place()
    g = other(s)
    a = z + core * (y - z)
    b = y + core * (z - y)
    mate = (s + 1 - 2 * core, h)

    first, loads = [], []
    for p in range(2):
        theirs = pl.ds(pl.multiple_of(p * HALF + (1 - core) * 384, 128), 384)
        ours = pl.ds(pl.multiple_of(p * HALF + core * 384, 128), 384)
        first.append(remote(g_ref.at[:, :, theirs], got.at[pl.ds(3 * p, 3)], ss.at[p], sr.at[p], mate))
        loads.append(pltpu.make_async_copy(g_ref.at[:, :, ours], own.at[pl.ds(3 * p, 3)], ls.at[p]))
    for copy in first + loads:
        copy.start()
    results = []
    for t, (src, dst) in enumerate(((x_ref, xo), (e_ref, eo))):
        for c in range(2):
            results.append(remote(src.at[:, :, pl.ds(c * HALF, HALF)], dst.at[pl.ds(2 * h, 2)], rs.at[t, c], rr.at[t, h], (g, c)))
    for copy in results:
        copy.start()
    for copy in first:
        copy.wait_recv()
    for copy in loads:
        copy.wait()

    def rowblock(r):
        return pl.ds(pl.multiple_of(r * 48, 48), 48)

    for n in range(6):
        @pl.loop(0, 32)
        def _(r):
            zz, yy = lax.rem(r // 4, 4), lax.rem(r, 4)
            total = own[n, rowblock(r), :].astype(f32) + got[n, rowblock(r), :].astype(f32)
            part[n, r // 16, zz + core * (yy - zz), yy + core * (zz - yy)] = total.astype(bf16)

    def relay(view, here, peer, t, u, base, loop):
        at = [lax.rem(here + k, 4) for k in range(4)]
        copies = [
            remote(view(0, 3, at[2]), t.at[0], ss.at[base], sr.at[base], peer(at[1])),
            remote(view(3, 3, at[2]), t.at[1], ss.at[base + 1], sr.at[base + 1], peer(at[3])),
        ]
        for copy in copies:
            copy.start()
        more = []
        for side, k in ((0, 1), (1, 3)):
            copies[side].wait_recv()
            loop(lambda i, j: add(view(3 * side, 3, at[k]), t.at[side], i, j), 3)
            more.append(remote(view(0, 6, at[k]), u.at[side], ss.at[base + 2 + side], sr.at[base + 2 + side], peer(at[k])))
            more[-1].start()
        for copy in more:
            copy.wait_recv()
        return copies + more

    def add(dst, src, i, j):
        dst[i, j] = (dst[i, j].astype(f32) + src[i, j].astype(f32)).astype(bf16)

    def loop1(fn, n):
        for i in range(n):
            @pl.loop(0, 8)
            def _(j):
                fn((i, j // 4, lax.rem(j, 4)), None)

    def add1(dst, src, i, j):
        dst[i] = (dst[i].astype(f32) + src[i].astype(f32)).astype(bf16)

    add = add1
    sent = relay(lambda lo, n, d: part.at[pl.ds(lo, n), :, :, d], b, lambda d: (line(core, low, a, d), h), t1, u1, 2, loop1)

    for n in range(6):
        @pl.loop(0, 8)
        def _(j):
            i, q = j // 4, lax.rem(j, 4)
            total = part[n, i, q, b].astype(f32) + u1[0, n, i, q].astype(f32) + u1[1, n, i, q].astype(f32)
            mid[n, i, q] = total.astype(bf16)

    def loop2(fn, n):
        for i in range(n):
            for j in range(2):
                fn((i, j), None)

    sent += relay(lambda lo, n, d: mid.at[pl.ds(lo, n), :, d], a, lambda d: (line(core, low, d, b), h), t2, u2, 6, loop2)
    for n in range(6):
        for i in range(2):
            total = mid[n, i, a].astype(f32) + u2[0, n, i].astype(f32) + u2[1, n, i].astype(f32)
            end[n, i] = total.astype(bf16)

    here = 2 * h + low
    direct = []
    for k in (1, 3, 2):
        d = lax.rem(here + k, 4)
        dh, dl = d // 2, lax.rem(d, 2)
        direct.append(remote(end.at[pl.ds(3 * dh, 3), dl], v3.at[k - 1], ss.at[10 + k - 1], sr.at[10 + k - 1], (dl * 32 + z * 8 + y * 2 + core, dh)))
    for copy in direct:
        copy.start()
    for copy in direct:
        copy.wait_recv()
    for n in range(3):
        fin[n] = end[3 * h + n, low].astype(f32) + v3[0, n].astype(f32) + v3[1, n].astype(f32) + v3[2, n].astype(f32)
    keep = pl.ds(pl.multiple_of(core * 24, 8), 24)
    give = pl.ds(pl.multiple_of((1 - core) * 24, 8), 24)
    final = remote(fin.at[:, give], swap, ss.at[13], sr.at[13], mate)
    final.start()
    mg[:, :, pl.ds(pl.multiple_of(core * 384, 128), 384)] = fin[:, keep, :]
    final.wait_recv()
    mg[:, :, pl.ds(pl.multiple_of((1 - core) * 384, 128), 384)] = swap[...]

    for t, (src, dst) in enumerate(((x_ref, xo), (e_ref, eo))):
        for c in range(2):
            remote(src.at[:, :, 0:HALF], dst.at[pl.ds(2 * c, 2)], rs.at[t, 0], rr.at[t, c], (g, 0)).wait_recv()
    for copy in results + first + sent + direct + [final]:
        copy.wait_send()


def scatter(x, e, grads):
    D = pltpu.SemaphoreType.DMA
    V = pltpu.VMEM
    return pl.pallas_call(
        out_kernel,
        out_shape=(
            jax.ShapeDtypeStruct((4, BINS, HALF), bf16),
            jax.ShapeDtypeStruct((4, BINS, HALF), bf16),
            jax.ShapeDtypeStruct((3, 24, HALF), f32),
        ),
        in_specs=[ANY] * 3,
        out_specs=(ANY, ANY, pl.BlockSpec(memory_space=pltpu.VMEM)),
        scratch_shapes=[
            V((6, FULL, 384), bf16), V((6, FULL, 384), bf16), V((6, 2, 4, 4, 48, 384), bf16),
            V((2, 3, 2, 4, 48, 384), bf16), V((2, 6, 2, 4, 48, 384), bf16), V((6, 2, 4, 48, 384), bf16),
            V((2, 3, 2, 48, 384), bf16), V((2, 6, 2, 48, 384), bf16), V((6, 2, 48, 384), bf16),
            V((3, 3, 48, 384), bf16), V((3, 48, 384), f32), V((3, 24, 384), f32),
            D((2, 2)), D((2, 2)), D((14,)), D((14,)), D((2,)),
        ],
        compiler_params=pltpu.CompilerParams(has_side_effects=True, vmem_limit_bytes=56 << 20),
    )(x, e, grads)


def gelu_parts(pre):
    half = 0.5 * (1.0 + lax.erf(pre * 0.7071067811865476))
    return pre * half, half + pre * jnp.exp(-0.5 * pre * pre) * 0.3989422804014327


def taps(value, d):
    n = value.shape[1]
    wide = jnp.pad(value.astype(f32), ((0, 0), (d, d), (0, 0)))
    return wide[:, 0:n], wide[:, d : d + n], wide[:, 2 * d : 2 * d + n]


def on_device(inputs, kernels, mixers, cotangent):
    s = lax.axis_index("seq")
    g = other(s)
    xg, eg, mix, kg = gather(inputs, cotangent, mixers, kernels.reshape(9, HALF))
    kernel = jnp.concatenate([kg[0], kg[1]], axis=1).reshape(3, 3, FULL)

    def inside(halo):
        at = g * BINS - halo + jnp.arange(BINS + 2 * halo)
        return ((at >= 0) & (at < 64 * BINS))[None, :, None]

    xin, ein = inside(XH), inside(EH)
    zero = jnp.zeros((), bf16)
    x = jnp.where(xin, xg, zero)
    own = slice(XH, XH + BINS)
    acts, slopes = [], []
    for blk, d in enumerate(dilations):
        lowt, midt, hight = taps(x, d)
        pre = kernel[blk, 0] * lowt + kernel[blk, 1] * midt + kernel[blk, 2] * hight
        act, slope = gelu_parts(pre)
        act = act.astype(bf16)
        acts.append(act[:, own].reshape(-1, FULL))
        slopes.append(slope[:, XH - EH : XH + BINS + EH])
        if blk == 2:
            act, x = act[:, own], x[:, own]
        n = act.shape[1]
        mixed = jnp.dot(act.reshape(-1, FULL), mix[blk], preferred_element_type=f32).reshape(2, n, FULL)
        x = (x.astype(f32) + mixed).astype(bf16)
        if blk < 2:
            x = jnp.where(xin, x, zero)
    out = x
    e = jnp.where(ein, eg, zero)
    grads = [None] * 3
    mine = slice(EH, EH + BINS)
    for blk in (2, 1, 0):
        d = dilations[blk]
        flat = e.reshape(-1, FULL)
        back = jnp.einsum("rj,cj->rc", flat, mix[blk], preferred_element_type=f32).reshape(e.shape)
        slope = jnp.where(ein, (back * slopes[blk]).astype(bf16), zero)
        grads[blk] = (
            jnp.einsum("rc,rj->cj", acts[blk], e[:, mine].reshape(-1, FULL), preferred_element_type=f32) * (1.0 / 256.0)
        ).astype(bf16)
        lowt, midt, hight = taps(slope, d)
        e = (e.astype(f32) + kernel[blk, 0] * hight + kernel[blk, 1] * midt + kernel[blk, 2] * lowt).astype(bf16)
    return scatter(out, e[:, mine], jnp.stack(grads))


def solution(mesh):
    return jax.shard_map(
        on_device,
        mesh=mesh,
        in_specs=(P(None, "seq", "ch"), P(None, None, "ch"), P(None, None, "ch"), P(None, "seq", "ch")),
        out_specs=(P(None, "seq", "ch"), P(None, "seq", "ch"), P(None, "seq", "ch")),
        check_vma=False,
    )
```

```python
import jax
import jax.numpy as jnp
from jax import lax
from jax.experimental import pallas as pl
from jax.experimental.pallas import tpu as pltpu
from jax.sharding import PartitionSpec as P

dilations = (2, 4, 8)
MESH = pl.DeviceIdType.MESH
ANY = pl.BlockSpec(memory_space=pl.ANY)
bf16, f32 = jnp.bfloat16, jnp.float32
XH, EH = 32, 16
BINS, HALF, FULL = 256, 768, 1536


def place():
    s = lax.axis_index("seq")
    h = lax.axis_index("ch")
    core = lax.rem(s, 2)
    y = lax.rem(s // 2, 4)
    z = lax.rem(s // 8, 4)
    return s, h, s // 32, z, y, core


def other(s):
    return lax.rem(s + 32, 64)


def line(core, low, a, b):
    z = a + core * (b - a)
    y = b + core * (a - b)
    return low * 32 + z * 8 + y * 2 + core


def remote(src, dst, send, recv, to):
    return pltpu.make_async_remote_copy(
        src_ref=src, dst_ref=dst, send_sem=send, recv_sem=recv, device_id=to, device_id_type=MESH
    )


def in_kernel(x_ref, e_ref, m_ref, k_ref, xo, eo, mo, ko, buf, xs, xr, ms, mr, ls):
    s, h, low, z, y, core = place()
    g = other(s)
    cols = pl.ds(pl.multiple_of(h * HALF, HALF), HALF)
    opp = pl.ds(pl.multiple_of((1 - h) * HALF, HALF), HALF)
    a = z + core * (y - z)
    b = y + core * (z - y)
    piece = core * 16 + a * 4 + b

    def rows(first, count):
        return pl.ds(pl.multiple_of(first * 48, 48), count * 48)

    mine = m_ref.at[:, rows(piece, 1), :]
    first = remote(mine, mo.at[:, rows(piece, 1), cols], ms.at[0], mr.at[0], (g, 1 - h))
    first.start()
    kcopy = remote(k_ref, ko.at[h], ms.at[1], mr.at[1], (g, 1 - h))
    kcopy.start()

    sends = []
    for t, (src, dst, halo) in enumerate(((x_ref, xo, XH), (e_ref, eo, EH))):
        for p in range(2):
            pair = pl.ds(2 * p, 2)
            sends.append((None, remote(src.at[pair], dst.at[:, halo : halo + BINS, cols], xs.at[t, p, 0], xr.at[t, h, 0], (g, p))))
            sends.append((s < 63, remote(
                src.at[pair, BINS - halo : BINS], dst.at[:, 0:halo, cols], xs.at[t, p, 1], xr.at[t, h, 1], (other(lax.rem(s + 1, 64)), p))))
            sends.append((s > 0, remote(
                src.at[pair, 0:halo], dst.at[:, halo + BINS : 2 * halo + BINS, cols], xs.at[t, p, 2], xr.at[t, h, 2], (other(lax.rem(s + 63, 64)), p))))
    for cond, copy in sends:
        if cond is None:
            copy.start()
        else:
            pl.when(cond)(copy.start)
    load = pltpu.make_async_copy(m_ref, buf, ls.at[0])
    load.start()
    klocal = pltpu.make_async_copy(k_ref, ko.at[h], ls.at[1])
    klocal.start()

    load.wait()
    local = pltpu.make_async_copy(buf, mo.at[:, :, cols], ls.at[0])
    local.start()

    def spread(step, count, start, peer):
        copies = []
        for k in (1, 3, 2):
            copies.append(remote(
                mo.at[:, rows(start, count), opp], mo.at[:, rows(start, count), opp], ms.at[2 + step * 3 + k - 1], mr.at[2 + step * 3 + k - 1], peer(k)))
        for copy in copies:
            copy.start()
        for copy in copies:
            copy.wait_recv()
        return copies

    remote(mine, mo.at[:, rows(piece, 1), opp], ms.at[0], mr.at[0], (g, 1 - h)).wait_recv()
    step1 = spread(0, 1, piece, lambda k: (line(core, low, a, lax.rem(b + k, 4)), h))
    step2 = spread(1, 4, core * 16 + a * 4, lambda k: (line(core, low, lax.rem(a + k, 4), b), h))
    last = remote(mo.at[:, rows(core * 16, 16), opp], mo.at[:, rows(core * 16, 16), opp], ms.at[8], mr.at[8], (s + 1 - 2 * core, h))
    last.start()
    last.wait_recv()

    for t, (src, dst, halo) in enumerate(((x_ref, xo, XH), (e_ref, eo, EH))):
        for c in range(2):
            half = pl.ds(c * HALF, HALF)
            remote(src.at[0:2], dst.at[:, halo : halo + BINS, half], xs.at[t, 0, 0], xr.at[t, c, 0], (g, 0)).wait_recv()
            pl.when(g > 0)(remote(src.at[0:2, 0:halo], dst.at[:, 0:halo, half], xs.at[t, 0, 1], xr.at[t, c, 1], (g, 0)).wait_recv)
            pl.when(g < 63)(remote(src.at[0:2, 0:halo], dst.at[:, 0:halo, half], xs.at[t, 0, 2], xr.at[t, c, 2], (g, 0)).wait_recv)
    kcopy.wait_recv()
    local.wait()
    klocal.wait()
    for cond, copy in sends:
        if cond is None:
            copy.wait_send()
        else:
            pl.when(cond)(copy.wait_send)
    for copy in [first, kcopy, last, *step1, *step2]:
        copy.wait_send()


def gather(x, e, m, k):
    D = pltpu.SemaphoreType.DMA
    return pl.pallas_call(
        in_kernel,
        out_shape=(
            jax.ShapeDtypeStruct((2, BINS + 2 * XH, FULL), bf16),
            jax.ShapeDtypeStruct((2, BINS + 2 * EH, FULL), bf16),
            jax.ShapeDtypeStruct((3, FULL, FULL), bf16),
            jax.ShapeDtypeStruct((2, 9, HALF), f32),
        ),
        in_specs=[ANY] * 4,
        out_specs=(ANY,) * 4,
        scratch_shapes=[pltpu.VMEM((3, FULL, HALF), bf16), D((2, 2, 3)), D((2, 2, 3)), D((9,)), D((9,)), D((2,))],
        compiler_params=pltpu.CompilerParams(has_side_effects=True),
    )(x, e, m, k)


def out_kernel(x_ref, e_ref, g_ref, xo, eo, mg, own, got, part, t1, u1, mid, t2, u2, end, v3, fin, swap, rs, rr, ss, sr, ls):
    s, h, low, z, y, core = place()
    g = other(s)
    a = z + core * (y - z)
    b = y + core * (z - y)
    mate = (s + 1 - 2 * core, h)

    first, loads = [], []
    for p in range(2):
        theirs = pl.ds(pl.multiple_of(p * HALF + (1 - core) * 384, 128), 384)
        ours = pl.ds(pl.multiple_of(p * HALF + core * 384, 128), 384)
        first.append(remote(g_ref.at[:, :, theirs], got.at[pl.ds(3 * p, 3)], ss.at[p], sr.at[p], mate))
        loads.append(pltpu.make_async_copy(g_ref.at[:, :, ours], own.at[pl.ds(3 * p, 3)], ls.at[p]))
    for copy in first + loads:
        copy.start()
    results = []
    for t, (src, dst) in enumerate(((x_ref, xo), (e_ref, eo))):
        for c in range(2):
            results.append(remote(src.at[:, :, pl.ds(c * HALF, HALF)], dst.at[pl.ds(2 * h, 2)], rs.at[t, c], rr.at[t, h], (g, c)))
    for copy in results:
        copy.start()
    for copy in first:
        copy.wait_recv()
    for copy in loads:
        copy.wait()

    def rowblock(r):
        return pl.ds(pl.multiple_of(r * 48, 48), 48)

    for n in range(6):
        @pl.loop(0, 32)
        def _(r):
            zz, yy = lax.rem(r // 4, 4), lax.rem(r, 4)
            total = own[n, rowblock(r), :].astype(f32) + got[n, rowblock(r), :].astype(f32)
            part[n, r // 16, zz + core * (yy - zz), yy + core * (zz - yy)] = total.astype(bf16)

    def relay(view, here, peer, t, u, base, loop):
        at = [lax.rem(here + k, 4) for k in range(4)]
        copies = [
            remote(view(0, 3, at[2]), t.at[0], ss.at[base], sr.at[base], peer(at[1])),
            remote(view(3, 3, at[2]), t.at[1], ss.at[base + 1], sr.at[base + 1], peer(at[3])),
        ]
        for copy in copies:
            copy.start()
        more = []
        for side, k in ((0, 1), (1, 3)):
            copies[side].wait_recv()
            loop(lambda i, j: add(view(3 * side, 3, at[k]), t.at[side], i, j), 3)
            more.append(remote(view(0, 6, at[k]), u.at[side], ss.at[base + 2 + side], sr.at[base + 2 + side], peer(at[k])))
            more[-1].start()
        for copy in more:
            copy.wait_recv()
        return copies + more

    def add(dst, src, i, j):
        dst[i, j] = (dst[i, j].astype(f32) + src[i, j].astype(f32)).astype(bf16)

    def loop1(fn, n):
        for i in range(n):
            @pl.loop(0, 8)
            def _(j):
                fn((i, j // 4, lax.rem(j, 4)), None)

    def add1(dst, src, i, j):
        dst[i] = (dst[i].astype(f32) + src[i].astype(f32)).astype(bf16)

    add = add1
    sent = relay(lambda lo, n, d: part.at[pl.ds(lo, n), :, :, d], b, lambda d: (line(core, low, a, d), h), t1, u1, 2, loop1)

    for n in range(6):
        @pl.loop(0, 8)
        def _(j):
            i, q = j // 4, lax.rem(j, 4)
            total = part[n, i, q, b].astype(f32) + u1[0, n, i, q].astype(f32) + u1[1, n, i, q].astype(f32)
            mid[n, i, q] = total.astype(bf16)

    def loop2(fn, n):
        for i in range(n):
            for j in range(2):
                fn((i, j), None)

    sent += relay(lambda lo, n, d: mid.at[pl.ds(lo, n), :, d], a, lambda d: (line(core, low, d, b), h), t2, u2, 6, loop2)
    for n in range(6):
        for i in range(2):
            total = mid[n, i, a].astype(f32) + u2[0, n, i].astype(f32) + u2[1, n, i].astype(f32)
            end[n, i] = total.astype(bf16)

    here = 2 * h + low
    direct = []
    for k in (1, 3, 2):
        d = lax.rem(here + k, 4)
        dh, dl = d // 2, lax.rem(d, 2)
        direct.append(remote(end.at[pl.ds(3 * dh, 3), dl], v3.at[k - 1], ss.at[10 + k - 1], sr.at[10 + k - 1], (dl * 32 + z * 8 + y * 2 + core, dh)))
    for copy in direct:
        copy.start()
    for copy in direct:
        copy.wait_recv()
    for n in range(3):
        fin[n] = end[3 * h + n, low].astype(f32) + v3[0, n].astype(f32) + v3[1, n].astype(f32) + v3[2, n].astype(f32)
    keep = pl.ds(pl.multiple_of(core * 24, 8), 24)
    give = pl.ds(pl.multiple_of((1 - core) * 24, 8), 24)
    final = remote(fin.at[:, give], swap, ss.at[13], sr.at[13], mate)
    final.start()
    mg[:, :, pl.ds(pl.multiple_of(core * 384, 128), 384)] = fin[:, keep, :]
    final.wait_recv()
    mg[:, :, pl.ds(pl.multiple_of((1 - core) * 384, 128), 384)] = swap[...]

    for t, (src, dst) in enumerate(((x_ref, xo), (e_ref, eo))):
        for c in range(2):
            remote(src.at[:, :, 0:HALF], dst.at[pl.ds(2 * c, 2)], rs.at[t, 0], rr.at[t, c], (g, 0)).wait_recv()
    for copy in results + first + sent + direct + [final]:
        copy.wait_send()


def scatter(x, e, grads):
    D = pltpu.SemaphoreType.DMA
    V = pltpu.VMEM
    return pl.pallas_call(
        out_kernel,
        out_shape=(
            jax.ShapeDtypeStruct((4, BINS, HALF), bf16),
            jax.ShapeDtypeStruct((4, BINS, HALF), bf16),
            jax.ShapeDtypeStruct((3, 24, HALF), f32),
        ),
        in_specs=[ANY] * 3,
        out_specs=(ANY, ANY, pl.BlockSpec(memory_space=pltpu.VMEM)),
        scratch_shapes=[
            V((6, FULL, 384), bf16), V((6, FULL, 384), bf16), V((6, 2, 4, 4, 48, 384), bf16),
            V((2, 3, 2, 4, 48, 384), bf16), V((2, 6, 2, 4, 48, 384), bf16), V((6, 2, 4, 48, 384), bf16),
            V((2, 3, 2, 48, 384), bf16), V((2, 6, 2, 48, 384), bf16), V((6, 2, 48, 384), bf16),
            V((3, 3, 48, 384), bf16), V((3, 48, 384), f32), V((3, 24, 384), f32),
            D((2, 2)), D((2, 2)), D((14,)), D((14,)), D((2,)),
        ],
        compiler_params=pltpu.CompilerParams(has_side_effects=True, vmem_limit_bytes=56 << 20),
    )(x, e, grads)


def gelu_parts(pre):
    half = 0.5 * (1.0 + lax.erf(pre * 0.7071067811865476))
    return pre * half, half + pre * jnp.exp(-0.5 * pre * pre) * 0.3989422804014327


def taps(value, d):
    n = value.shape[1]
    wide = jnp.pad(value.astype(f32), ((0, 0), (d, d), (0, 0)))
    return wide[:, 0:n], wide[:, d : d + n], wide[:, 2 * d : 2 * d + n]


def on_device(inputs, kernels, mixers, cotangent):
    s = lax.axis_index("seq")
    g = other(s)
    xg, eg, mix, kg = gather(inputs, cotangent, mixers, kernels.reshape(9, HALF))
    kernel = jnp.concatenate([kg[0], kg[1]], axis=1).reshape(3, 3, FULL)

    def inside(halo):
        at = g * BINS - halo + jnp.arange(BINS + 2 * halo)
        return ((at >= 0) & (at < 64 * BINS))[None, :, None]

    xin, ein = inside(XH), inside(EH)
    zero = jnp.zeros((), bf16)
    x = jnp.where(xin, xg, zero)
    own = slice(XH, XH + BINS)
    acts, slopes = [], []
    for blk, d in enumerate(dilations):
        lowt, midt, hight = taps(x, d)
        pre = kernel[blk, 0] * lowt + kernel[blk, 1] * midt + kernel[blk, 2] * hight
        act, slope = gelu_parts(pre)
        act = act.astype(bf16)
        acts.append(act[:, own].reshape(-1, FULL))
        slopes.append(slope[:, XH - EH : XH + BINS + EH])
        if blk == 2:
            act, x = act[:, own], x[:, own]
        n = act.shape[1]
        mixed = jnp.dot(act.reshape(-1, FULL), mix[blk], preferred_element_type=f32).reshape(2, n, FULL)
        x = (x.astype(f32) + mixed).astype(bf16)
        if blk < 2:
            x = jnp.where(xin, x, zero)
    out = x
    e = jnp.where(ein, eg, zero)
    grads = [None] * 3
    mine = slice(EH, EH + BINS)
    for blk in (2, 1, 0):
        d = dilations[blk]
        flat = e.reshape(-1, FULL)
        back = jnp.einsum("rj,cj->rc", flat, mix[blk], preferred_element_type=f32).reshape(e.shape)
        slope = jnp.where(ein, (back * slopes[blk]).astype(bf16), zero)
        grads[blk] = (
            jnp.einsum("rc,rj->cj", acts[blk], e[:, mine].reshape(-1, FULL), preferred_element_type=f32) * (1.0 / 256.0)
        ).astype(bf16)
        lowt, midt, hight = taps(slope, d)
        e = (e.astype(f32) + kernel[blk, 0] * hight + kernel[blk, 1] * midt + kernel[blk, 2] * lowt).astype(bf16)
    return scatter(out, e[:, mine], jnp.stack(grads))


def solution(mesh):
    return jax.shard_map(
        on_device,
        mesh=mesh,
        in_specs=(P(None, "seq", "ch"), P(None, None, "ch"), P(None, None, "ch"), P(None, "seq", "ch")),
        out_specs=(P(None, "seq", "ch"), P(None, "seq", "ch"), P(None, "seq", "ch")),
        check_vma=False,
    )
```

```python
import jax
import jax.numpy as jnp
from jax import lax
from jax.experimental import pallas as pl
from jax.experimental.pallas import tpu as pltpu
from jax.sharding import PartitionSpec as P

dilations = (2, 4, 8)
MESH = pl.DeviceIdType.MESH
ANY = pl.BlockSpec(memory_space=pl.ANY)
bf16, f32 = jnp.bfloat16, jnp.float32
XH, EH = 32, 16
BINS, HALF, FULL = 256, 768, 1536
XN, EN = BINS + 2 * XH, BINS + 2 * EH
ROWS = 48
TILE = 128


def place():
    s = lax.axis_index("seq")
    h = lax.axis_index("ch")
    core = lax.rem(s, 2)
    y = lax.rem(s // 2, 4)
    z = lax.rem(s // 8, 4)
    return s, h, s // 32, z, y, core


def other(s):
    return lax.rem(s + 32, 64)


def line(core, low, a, b):
    z = a + core * (b - a)
    y = b + core * (a - b)
    return low * 32 + z * 8 + y * 2 + core


def remote(src, dst, send, recv, to):
    return pltpu.make_async_remote_copy(
        src_ref=src, dst_ref=dst, send_sem=send, recv_sem=recv, device_id=to, device_id_type=MESH
    )


def lanes(start, size, step=128):
    return pl.ds(pl.multiple_of(start, step), size)


def body(
    x_ref, e_ref, m_ref, k_ref, xo, eo, mg,
    xv, ev, acts, slopes, down, mv, kv, give, got, part, t1, u1, mid, t2, u2, end, v3, fin, swap,
    xs, xr, ms, mr, ks, rs, rr, ss, sr, ls,
):
    s, h, low, z, y, core = place()
    g = other(s)
    a = z + core * (y - z)
    b = y + core * (z - y)
    mate = (s + 1 - 2 * core, h)
    here = 2 * h + low
    piece = core * 16 + a * 4 + b
    pending = []

    def start(copy, cond=None):
        pending.append((cond, copy))
        if cond is None:
            copy.start()
        else:
            pl.when(cond)(copy.start)
        return copy

    along_a = lambda k: (line(core, low, lax.rem(a + k, 4), b), h)
    along_b = lambda k: (line(core, low, a, lax.rem(b + k, 4)), h)

    def along_x(k):
        d = lax.rem(here + k, 4)
        return (lax.rem(d, 2) * 32 + z * 8 + y * 2 + core, d // 2)

    barrier = pltpu.get_barrier_semaphore()
    peers = [(g, 0), (g, 1), (s, 1 - h), mate]
    peers += [(lax.rem(g + d, 64), p) for d in (1, 63) for p in range(2)]
    peers += [line_of(k) for line_of in (along_a, along_b) for k in (1, 2, 3)]
    for peer in peers:
        pl.semaphore_signal(barrier, inc=1, device_id=peer, device_id_type=MESH)
    own_mix = pltpu.make_async_copy(m_ref, mv.at[:, h], ls.at[0])
    own_mix.start()
    pl.semaphore_wait(barrier, len(peers))

    def rows(first, count):
        return pl.ds(pl.multiple_of(first * ROWS, ROWS), count * ROWS)

    def hop(blk):
        return remote(m_ref.at[blk, rows(piece, 1), :], mv.at[blk, h, rows(piece, 1)], ms.at[blk, 0], mr.at[blk, 0], (g, 1 - h))

    sides = ((x_ref, xv, XH), (e_ref, ev, EH))

    def send_in(t, q):
        src, dst, halo = sides[t]
        cols = lanes(h * HALF, HALF)
        for p in range(2):
            at = (t, q, p)
            start(remote(src.at[2 * p + q], dst.at[q, halo : halo + BINS, cols], xs.at[*at, 0], xr.at[t, q, h, 0], (g, p)))
        for p in range(2):
            at = (t, q, p)
            start(remote(src.at[2 * p + q, BINS - halo : BINS], dst.at[q, 0:halo, cols], xs.at[*at, 1], xr.at[t, q, h, 1], (other(lax.rem(s + 1, 64)), p)), s < 63)
            start(remote(src.at[2 * p + q, 0:halo], dst.at[q, halo + BINS : BINS + 2 * halo, cols], xs.at[*at, 2], xr.at[t, q, h, 2], (other(lax.rem(s + 63, 64)), p)), s > 0)

    def wait_in(t, q):
        src, dst, halo = sides[t]
        for c in range(2):
            half = pl.ds(c * HALF, HALF)
            remote(src.at[0], dst.at[q, halo : halo + BINS, half], xs.at[t, q, 0, 0], xr.at[t, q, c, 0], (g, 0)).wait_recv()
            pl.when(g > 0)(remote(src.at[0, 0:halo], dst.at[q, 0:halo, half], xs.at[t, q, 0, 1], xr.at[t, q, c, 1], (g, 0)).wait_recv)
            pl.when(g < 63)(remote(src.at[0, 0:halo], dst.at[q, halo + BINS : BINS + 2 * halo, half], xs.at[t, q, 0, 2], xr.at[t, q, c, 2], (g, 0)).wait_recv)

    def spread(blk, step, first, count, peer):
        for k in (1, 3, 2):
            at = (blk, step * 3 + k)
            start(remote(mv.at[blk, 1 - h, rows(first, count)], mv.at[blk, 1 - h, rows(first, count)], ms.at[*at], mr.at[*at], peer(k)))

    def spread_wait(blk, step, count, peer):
        for k in (1, 3, 2):
            at = (blk, step * 3 + k)
            remote(mv.at[blk, 1 - h, 0 : count * ROWS], mv.at[blk, 1 - h, 0 : count * ROWS], ms.at[*at], mr.at[*at], peer(k)).wait_recv()

    def across(blk):
        at = mv.at[blk, 1 - h, rows(core * 16, 16)]
        return remote(at, at, ms.at[blk, 7], mr.at[blk, 7], mate)

    start(hop(0))
    kcopy = start(remote(k_ref, kv.at[h], ks.at[0], ks.at[1], (g, 1 - h)))
    klocal = pltpu.make_async_copy(k_ref, kv.at[h], ls.at[1])
    klocal.start()
    send_in(0, 0)
    start(hop(1))
    start(hop(2))
    send_in(0, 1)
    send_in(1, 0)
    send_in(1, 1)
    for blk in range(3):
        hop(blk).wait_recv()
        spread(blk, 0, piece, 1, along_b)
    for blk in range(3):
        spread_wait(blk, 0, 1, along_b)
        spread(blk, 1, core * 16 + a * 4, 4, along_a)

    def zero_edges(ref, q, halo):
        pl.when(g == 0)(lambda: put_zero(ref, q, 0, halo))
        pl.when(g == 63)(lambda: put_zero(ref, q, BINS + halo, halo))

    def put_zero(ref, q, first, count):
        ref[q, first : first + count, :] = jnp.zeros((count, FULL), bf16)

    for q in range(2):
        zero_edges(xv, q, XH)
        zero_edges(ev, q, EH)

    def weight(blk, tap, part_of, at):
        return kv[part_of, 3 * blk + tap : 3 * blk + tap + 1, lanes(at * TILE, TILE)]

    def column_tiles(fn):
        for part_of in range(2):
            @pl.loop(0, HALF // TILE)
            def _(j):
                fn(part_of, j, lanes(part_of * HALF + j * TILE, TILE))

    def forward(blk, q):
        d = dilations[blk]

        def tile(part_of, j, cols):
            value = xv[q, :, cols].astype(f32)
            pre = (
                weight(blk, 0, part_of, j) * pltpu.roll(value, d, 0)
                + weight(blk, 1, part_of, j) * value
                + weight(blk, 2, part_of, j) * pltpu.roll(value, XN - d, 0)
            )
            half = 0.5 * (1.0 + lax.erf(pre * 0.7071067811865476))
            acts[blk, q, :, cols] = (pre * half).astype(bf16)
            slope = half + pre * jnp.exp(-0.5 * pre * pre) * 0.3989422804014327
            slopes[blk, q, :, cols] = slope[XH - EH : XH + BINS + EH].astype(bf16)

        column_tiles(tile)

    def mix(blk, q):
        span = pl.ds(0, XN) if blk < 2 else pl.ds(XH, BINS)
        for part_of in range(2):
            @pl.loop(0, HALF // 256)
            def _(j):
                cols = lanes(part_of * HALF + j * 256, 256)
                mixed = jnp.dot(acts[blk, q, span, :], mv[blk, part_of, :, lanes(j * 256, 256)], preferred_element_type=f32)
                xv[q, span, cols] = (xv[q, span, cols].astype(f32) + mixed).astype(bf16)
        if blk < 2:
            zero_edges(xv, q, XH)

    def back(blk, q):
        @pl.loop(0, FULL // 256)
        def _(j):
            span = pl.ds(pl.multiple_of(j * 256, 256), 256)
            total = None
            for part_of in range(2):
                term = lax.dot_general(
                    ev[q, :, part_of * HALF : (part_of + 1) * HALF], mv[blk, part_of, span, :],
                    (((1,), (1,)), ((), ())), preferred_element_type=f32)
                total = term if total is None else total + term
            cols = lanes(j * 256, 256)
            down[q, :, cols] = (total * slopes[blk, q, :, cols].astype(f32)).astype(bf16)
        zero_edges(down, q, EH)

    def lower(blk, q):
        d = dilations[blk]

        def tile(part_of, j, cols):
            value = down[q, :, cols].astype(f32)
            total = (
                ev[q, :, cols].astype(f32)
                + weight(blk, 0, part_of, j) * pltpu.roll(value, EN - d, 0)
                + weight(blk, 1, part_of, j) * value
                + weight(blk, 2, part_of, j) * pltpu.roll(value, d, 0)
            )
            ev[q, :, cols] = total.astype(bf16)

        column_tiles(tile)

    def grads(blk):
        scale = 1.0 / 256.0
        for keep in (0, 1):
            theirs = core if keep else 1 - core
            for p in range(2):
                cols = lanes(p * HALF + theirs * 384, 384)

                @pl.loop(0, 4)
                def _(c):
                    total = None
                    for q in range(2):
                        term = lax.dot_general(
                            acts[blk, q, XH : XH + BINS, lanes(c * 384, 384)], ev[q, EH : EH + BINS, cols],
                            (((0,), (0,)), ((), ())), preferred_element_type=f32)
                        total = term if total is None else total + term
                    total = (total * scale).astype(bf16)
                    for r in range(8):
                        zz, yy = lax.rem(2 * c + r // 4, 4), r % 4
                        block = total[r * ROWS : (r + 1) * ROWS]
                        if keep:
                            part[blk, p, c // 2, zz + core * (yy - zz), yy + core * (zz - yy)] = block
                        else:
                            give[p, c // 2, zz + (1 - core) * (yy - zz), yy + (1 - core) * (zz - yy)] = block

    def add(dst, src):
        dst[...] = (dst[...].astype(f32) + src[...].astype(f32)).astype(bf16)

    def send(blk, n, src, dst, to):
        return start(remote(src, dst, ss.at[blk, n], sr.at[blk, n], to))

    def recv(blk, n, dst):
        remote(dst, dst, ss.at[blk, n], sr.at[blk, n], mate).wait_recv()

    pos = lambda here_, k: lax.rem(here_ + k, 4)

    def step0(blk):
        remote(give, got.at[blk], ss.at[blk, 0], sr.at[blk, 0], mate).start()

    def step1(blk):
        recv(blk, 0, got.at[blk])
        for p in range(2):
            @pl.loop(0, 32)
            def _(r):
                add(part.at[blk, p, r // 16, lax.rem(r // 4, 4), lax.rem(r, 4)], got.at[blk, p, r // 16, lax.rem(r // 4, 4), lax.rem(r, 4)])
        send(blk, 1, part.at[blk, 0, :, :, pos(b, 2)], t1.at[blk, 0], along_b(1))
        send(blk, 2, part.at[blk, 1, :, :, pos(b, 2)], t1.at[blk, 1], along_b(3))

    def step2(blk):
        for side, k in ((0, 1), (1, 3)):
            recv(blk, 1 + side, t1.at[blk, side])
            @pl.loop(0, 8)
            def _(r):
                add(part.at[blk, side, r // 4, lax.rem(r, 4), pos(b, k)], t1.at[blk, side, r // 4, lax.rem(r, 4)])
            send(blk, 3 + side, part.at[blk, :, :, :, pos(b, k)], u1.at[blk, side], along_b(k))

    def step3(blk):
        recv(blk, 3, u1.at[blk, 0])
        recv(blk, 4, u1.at[blk, 1])
        for p in range(2):
            @pl.loop(0, 8)
            def _(r):
                i, j = r // 4, lax.rem(r, 4)
                total = part[blk, p, i, j, b].astype(f32) + u1[blk, 0, p, i, j].astype(f32) + u1[blk, 1, p, i, j].astype(f32)
                mid[blk, p, i, j] = total.astype(bf16)
        send(blk, 5, mid.at[blk, 0, :, pos(a, 2)], t2.at[blk, 0], along_a(1))
        send(blk, 6, mid.at[blk, 1, :, pos(a, 2)], t2.at[blk, 1], along_a(3))

    def step4(blk):
        for side, k in ((0, 1), (1, 3)):
            recv(blk, 5 + side, t2.at[blk, side])
            for i in range(2):
                add(mid.at[blk, side, i, pos(a, k)], t2.at[blk, side, i])
            send(blk, 7 + side, mid.at[blk, :, :, pos(a, k)], u2.at[blk, side], along_a(k))

    def step5(blk):
        recv(blk, 7, u2.at[blk, 0])
        recv(blk, 8, u2.at[blk, 1])
        for p in range(2):
            for i in range(2):
                total = mid[blk, p, i, a].astype(f32) + u2[blk, 0, p, i].astype(f32) + u2[blk, 1, p, i].astype(f32)
                end[blk, p, i] = total.astype(bf16)
        for k in (1, 3, 2):
            d = pos(here, k)
            send(blk, 8 + k, end.at[blk, d // 2, lax.rem(d, 2)], v3.at[blk, k - 1], along_x(k))

    def step6(blk):
        for k in (1, 3, 2):
            recv(blk, 8 + k, v3.at[blk, k - 1])
        fin[blk] = end[blk, h, low].astype(f32) + v3[blk, 0].astype(f32) + v3[blk, 1].astype(f32) + v3[blk, 2].astype(f32)
        send(blk, 12, fin.at[blk, pl.ds(pl.multiple_of((1 - core) * 24, 8), 24)], swap.at[blk], mate)

    def step7(blk):
        mg[blk, :, lanes(core * 384, 384)] = fin[blk, pl.ds(pl.multiple_of(core * 24, 8), 24), :]
        recv(blk, 12, swap.at[blk])
        mg[blk, :, lanes((1 - core) * 384, 384)] = swap[blk]

    def give_sent(blk):
        remote(give, got.at[blk], ss.at[blk, 0], sr.at[blk, 0], mate).wait_send()

    def send_out(t, q):
        src, halo, dst = ((xv, XH, xo), (ev, EH, eo))[t]
        for c in range(2):
            start(remote(src.at[q, halo : halo + BINS, c * HALF : (c + 1) * HALF], dst.at[2 * h + q], rs.at[t, q, c], rr.at[t, q, h], (g, c)))

    for q in range(2):
        wait_in(0, q)
        if q == 0:
            klocal.wait()
            remote(k_ref, kv.at[1 - h], ks.at[0], ks.at[1], (g, 1 - h)).wait_recv()
        for blk in range(3):
            forward(blk, q)
            if q == 0:
                if blk == 0:
                    own_mix.wait()
                    for each in range(3):
                        spread_wait(each, 1, 4, along_a)
                        start(across(each))
                remote(mv.at[blk, 1 - h, 0 : 16 * ROWS], mv.at[blk, 1 - h, 0 : 16 * ROWS], ms.at[blk, 7], mr.at[blk, 7], mate).wait_recv()
            mix(blk, q)
        send_out(0, q)

    wait_in(1, 0)
    wait_in(1, 1)
    for blk in (2, 1, 0):
        if blk < 2:
            give_sent(blk + 1)
        grads(blk)
        step0(blk)
        if blk < 2:
            step3(blk + 1)
        if blk < 1:
            step6(blk + 2)
        for q in range(2):
            back(blk, q)
            lower(blk, q)
            if blk == 0:
                send_out(1, q)
            if q == 0:
                step1(blk)
                if blk < 2:
                    step4(blk + 1)
                if blk < 1:
                    step7(blk + 2)
        step2(blk)
        if blk < 2:
            step5(blk + 1)
    step3(0)
    step6(1)
    step4(0)
    step7(1)
    step5(0)
    step6(0)
    step7(0)

    for t, dst in enumerate((xo, eo)):
        for q in range(2):
            for c in range(2):
                remote(xv.at[q, 0:BINS, 0:HALF], dst.at[2 * c + q], rs.at[t, q, 0], rr.at[t, q, c], (g, 0)).wait_recv()
    give_sent(0)
    for cond, copy in pending:
        if cond is None:
            copy.wait_send()
        else:
            pl.when(cond)(copy.wait_send)


def on_device(inputs, kernels, mixers, cotangent):
    D = pltpu.SemaphoreType.DMA
    V = pltpu.VMEM
    return pl.pallas_call(
        body,
        out_shape=(
            jax.ShapeDtypeStruct((4, BINS, HALF), bf16),
            jax.ShapeDtypeStruct((4, BINS, HALF), bf16),
            jax.ShapeDtypeStruct((3, 24, HALF), f32),
        ),
        in_specs=[ANY] * 4,
        out_specs=(ANY, ANY, pl.BlockSpec(memory_space=pltpu.VMEM)),
        scratch_shapes=[
            V((2, XN, FULL), bf16), V((2, EN, FULL), bf16), V((3, 2, XN, FULL), bf16), V((3, 2, EN, FULL), bf16), V((2, EN, FULL), bf16),
            V((3, 2, FULL, HALF), bf16), V((2, 9, HALF), f32),
            V((2, 2, 4, 4, ROWS, 384), bf16), V((3, 2, 2, 4, 4, ROWS, 384), bf16), V((3, 2, 2, 4, 4, ROWS, 384), bf16),
            V((3, 2, 2, 4, ROWS, 384), bf16), V((3, 2, 2, 2, 4, ROWS, 384), bf16), V((3, 2, 2, 4, ROWS, 384), bf16),
            V((3, 2, 2, ROWS, 384), bf16), V((3, 2, 2, 2, ROWS, 384), bf16), V((3, 2, 2, ROWS, 384), bf16),
            V((3, 3, ROWS, 384), bf16), V((3, ROWS, 384), f32), V((3, 24, 384), f32),
            D((2, 2, 2, 3)), D((2, 2, 2, 3)), D((3, 8)), D((3, 8)), D((2,)), D((2, 2, 2)), D((2, 2, 2)), D((3, 13)), D((3, 13)), D((2,)),
        ],
        compiler_params=pltpu.CompilerParams(collective_id=0, has_side_effects=True, vmem_limit_bytes=60 << 20),
    )(inputs, cotangent, mixers, kernels.reshape(9, HALF))


def solution(mesh):
    return jax.shard_map(
        on_device,
        mesh=mesh,
        in_specs=(P(None, "seq", "ch"), P(None, None, "ch"), P(None, None, "ch"), P(None, "seq", "ch")),
        out_specs=(P(None, "seq", "ch"), P(None, "seq", "ch"), P(None, "seq", "ch")),
        check_vma=False,
    )
```

```python
import jax
import jax.numpy as jnp
from jax import lax
from jax.experimental import pallas as pl
from jax.experimental.pallas import tpu as pltpu
from jax.sharding import PartitionSpec as P

dilations = (2, 4, 8)
MESH = pl.DeviceIdType.MESH
ANY = pl.BlockSpec(memory_space=pl.ANY)
bf16, f32 = jnp.bfloat16, jnp.float32
XH, EH = 32, 16
BINS, HALF, FULL = 256, 768, 1536
XN, EN = BINS + 2 * XH, BINS + 2 * EH
ROWS = 48
TILE = 128


def place():
    s = lax.axis_index("seq")
    h = lax.axis_index("ch")
    core = lax.rem(s, 2)
    y = lax.rem(s // 2, 4)
    z = lax.rem(s // 8, 4)
    return s, h, s // 32, z, y, core


def other(s):
    return lax.rem(s + 32, 64)


def line(core, low, a, b):
    z = a + core * (b - a)
    y = b + core * (a - b)
    return low * 32 + z * 8 + y * 2 + core


def remote(src, dst, send, recv, to):
    return pltpu.make_async_remote_copy(
        src_ref=src, dst_ref=dst, send_sem=send, recv_sem=recv, device_id=to, device_id_type=MESH
    )


def lanes(start, size, step=128):
    return pl.ds(pl.multiple_of(start, step), size)


def body(
    x_ref, e_ref, m_ref, k_ref, xo, eo, mg,
    xv, ev, acts, slopes, down, mv, kv, give, got, part, t1, u1, mid, u2, end, v3, fin, swap,
    xs, xr, es, er, ms, mr, ks, rs, rr, ss, sr, ls,
):
    s, h, low, z, y, core = place()
    g = other(s)
    a = z + core * (y - z)
    b = y + core * (z - y)
    mate = (s + 1 - 2 * core, h)
    here = 2 * h + low
    piece = core * 16 + a * 4 + b
    pending = []

    def start(copy, cond=None):
        pending.append((cond, copy))
        if cond is None:
            copy.start()
        else:
            pl.when(cond)(copy.start)
        return copy

    along_a = lambda k: (line(core, low, lax.rem(a + k, 4), b), h)
    along_b = lambda k: (line(core, low, a, lax.rem(b + k, 4)), h)

    def along_x(k):
        d = lax.rem(here + k, 4)
        return (lax.rem(d, 2) * 32 + z * 8 + y * 2 + core, d // 2)

    barrier = pltpu.get_barrier_semaphore()
    peers = [(g, 0), (g, 1), (s, 1 - h), mate]
    peers += [(other(lax.rem(g + d, 64)), h) for d in (1, 63)]
    peers += [line_of(k) for line_of in (along_a, along_b) for k in (1, 2, 3)]
    for peer in peers:
        pl.semaphore_signal(barrier, inc=1, device_id=peer, device_id_type=MESH)
    pl.semaphore_wait(barrier, len(peers))

    def rows(first, count):
        return pl.ds(pl.multiple_of(first * ROWS, ROWS), count * ROWS)

    def hop(blk):
        return remote(m_ref.at[blk, rows(piece, 1), :], mv.at[blk, h, rows(piece, 1)], ms.at[blk, 0], mr.at[blk, 0], (g, 1 - h))

    sides = ((x_ref, xv, XH), (e_ref, ev, EH))

    def send_in(t, q):
        src, dst, halo = sides[t]
        for p in range(2):
            start(remote(src.at[2 * p + q], dst.at[q, halo : halo + BINS, lanes(h * HALF, HALF)], xs.at[t, q, p], xr.at[t, q, h], (g, p)))

    def wait_in(t, q):
        src, dst, halo = sides[t]
        for c in range(2):
            remote(src.at[0], dst.at[q, halo : halo + BINS, c * HALF : (c + 1) * HALF], xs.at[t, q, 0], xr.at[t, q, c], (g, 0)).wait_recv()
        for cond, copy in edges(t, q):
            pl.when(cond)(copy.start)

    def edges(t, q):
        src, dst, halo = sides[t]
        up, down_to = (other(lax.rem(g + 1, 64)), h), (other(lax.rem(g + 63, 64)), h)
        return (
            (g < 63, remote(dst.at[q, BINS : BINS + halo], dst.at[q, 0:halo], es.at[t, q, 0], er.at[t, q, 0], up)),
            (g > 0, remote(dst.at[q, halo : 2 * halo], dst.at[q, halo + BINS : 2 * halo + BINS], es.at[t, q, 1], er.at[t, q, 1], down_to)),
        )

    def edges_sent(t, q):
        for cond, copy in edges(t, q):
            pl.when(cond)(copy.wait_send)

    def wait_edges(t, q):
        src, dst, halo = sides[t]
        pl.when(g > 0)(remote(dst.at[q, 0:halo], dst.at[q, 0:halo], es.at[t, q, 0], er.at[t, q, 0], mate).wait_recv)
        pl.when(g < 63)(remote(dst.at[q, 0:halo], dst.at[q, halo + BINS : 2 * halo + BINS], es.at[t, q, 1], er.at[t, q, 1], mate).wait_recv)

    def spread(blk, step, first, count, peer):
        for k in (1, 3, 2):
            at = (blk, step * 3 + k)
            start(remote(mv.at[blk, 1 - h, rows(first, count)], mv.at[blk, 1 - h, rows(first, count)], ms.at[*at], mr.at[*at], peer(k)))

    def spread_wait(blk, step, count, peer):
        for k in (1, 3, 2):
            at = (blk, step * 3 + k)
            remote(mv.at[blk, 1 - h, 0 : count * ROWS], mv.at[blk, 1 - h, 0 : count * ROWS], ms.at[*at], mr.at[*at], peer(k)).wait_recv()

    def across(blk):
        at = mv.at[blk, 1 - h, rows(core * 16, 16)]
        return remote(at, at, ms.at[blk, 7], mr.at[blk, 7], mate)

    for blk in range(3):
        start(hop(blk))
    send_in(0, 0)
    kcopy = start(remote(k_ref, kv.at[h], ks.at[0], ks.at[1], (g, 1 - h)))
    klocal = pltpu.make_async_copy(k_ref, kv.at[h], ls.at[1])
    klocal.start()
    own_mix = pltpu.make_async_copy(m_ref, mv.at[:, h], ls.at[0])
    own_mix.start()

    def zero_edges(ref, q, halo):
        pl.when(g == 0)(lambda: put_zero(ref, q, 0, halo))
        pl.when(g == 63)(lambda: put_zero(ref, q, BINS + halo, halo))

    def put_zero(ref, q, first, count):
        ref[q, first : first + count, :] = jnp.zeros((count, FULL), bf16)

    for q in range(2):
        zero_edges(xv, q, XH)
        zero_edges(ev, q, EH)

    def weight(blk, tap, part_of, at):
        return kv[part_of, blk, tap : tap + 1, lanes(at * TILE, TILE)]

    def column_tiles(fn):
        for part_of in range(2):
            @pl.loop(0, HALF // TILE)
            def _(j):
                fn(part_of, j, lanes(part_of * HALF + j * TILE, TILE))

    def forward(blk, q):
        d = dilations[blk]

        def tile(part_of, j, cols):
            value = xv[q, :, cols].astype(f32)
            pre = (
                weight(blk, 0, part_of, j) * pltpu.roll(value, d, 0)
                + weight(blk, 1, part_of, j) * value
                + weight(blk, 2, part_of, j) * pltpu.roll(value, XN - d, 0)
            )
            half = 0.5 * (1.0 + lax.erf(pre * 0.7071067811865476))
            acts[blk, q, :, cols] = (pre * half).astype(bf16)
            slope = half + pre * jnp.exp(-0.5 * pre * pre) * 0.3989422804014327
            slopes[blk, q, :, cols] = slope[XH - EH : XH + BINS + EH].astype(bf16)

        column_tiles(tile)

    def mix(blk, q):
        span = pl.ds(0, XN) if blk < 2 else pl.ds(XH, BINS)
        @pl.loop(0, 2)
        def _(part_of):
            cols = lanes(part_of * HALF, HALF)
            mixed = jnp.dot(acts[blk, q, span, :], mv[blk, part_of], preferred_element_type=f32)
            xv[q, span, cols] = (xv[q, span, cols].astype(f32) + mixed).astype(bf16)

        if blk < 2:
            zero_edges(xv, q, XH)

    def back(blk, q):
        total = None
        for part_of in range(2):
            term = lax.dot_general(
                ev[q, :, part_of * HALF : (part_of + 1) * HALF], mv[blk, part_of],
                (((1,), (1,)), ((), ())), preferred_element_type=f32)
            total = term if total is None else total + term
        down[q] = (total * slopes[blk, q].astype(f32)).astype(bf16)
        zero_edges(down, q, EH)

    def lower(blk, q):
        d = dilations[blk]

        def tile(part_of, j, cols):
            value = down[q, :, cols].astype(f32)
            total = (
                ev[q, :, cols].astype(f32)
                + weight(blk, 0, part_of, j) * pltpu.roll(value, EN - d, 0)
                + weight(blk, 1, part_of, j) * value
                + weight(blk, 2, part_of, j) * pltpu.roll(value, d, 0)
            )
            ev[q, :, cols] = total.astype(bf16)

        column_tiles(tile)

    def product(blk, of, c):
        total = None
        for q in range(2):
            right = jnp.concatenate([ev[q, EH : EH + BINS, lanes(p * HALF + of * 384, 384)] for p in range(2)], axis=1)
            term = lax.dot_general(
                acts[blk, q, XH : XH + BINS, lanes(c * HALF, HALF)], right,
                (((0,), (0,)), ((), ())), preferred_element_type=f32)
            total = term if total is None else total + term
        return total * (1.0 / 256.0)

    def spot(of, r):
        zz, yy = r // 4, r % 4
        return zz + of * (yy - zz), yy + of * (zz - yy)

    def grads_give(blk):
        @pl.loop(0, 2)
        def _(c):
            total = product(blk, 1 - core, c).astype(bf16)
            for p in range(2):
                for r in range(16):
                    give[(p, c, *spot(1 - core, r))] = total[r * ROWS : (r + 1) * ROWS, p * 384 : (p + 1) * 384]

        remote(give, got.at[blk], ss.at[blk, 11], sr.at[blk, 11], mate).start()

    def grads_own(blk):
        recv(blk, 11, got.at[blk])

        @pl.loop(0, 2)
        def _(c):
            total = product(blk, core, c)
            for p in range(2):
                for r in range(16):
                    at = (blk, p, c, *spot(core, r))
                    part[at] = (total[r * ROWS : (r + 1) * ROWS, p * 384 : (p + 1) * 384] + got[at].astype(f32)).astype(bf16)

        for p in range(2):
            send(blk, p, part.at[blk, p, :, :, pos(b, 2)], t1.at[blk, p], along_b(1 + 2 * p))

    def add(dst, src):
        dst[...] = (dst[...].astype(f32) + src[...].astype(f32)).astype(bf16)

    def send(blk, n, src, dst, to):
        return start(remote(src, dst, ss.at[blk, n], sr.at[blk, n], to))

    def recv(blk, n, dst):
        remote(dst, dst, ss.at[blk, n], sr.at[blk, n], mate).wait_recv()

    pos = lambda here_, k: lax.rem(here_ + k, 4)

    def step2(blk):
        for side, k in ((0, 1), (1, 3)):
            recv(blk, side, t1.at[blk, side])

            @pl.loop(0, 8)
            def _(r):
                add(part.at[blk, side, r // 4, lax.rem(r, 4), pos(b, k)], t1.at[blk, side, r // 4, lax.rem(r, 4)])

            send(blk, 2 + side, part.at[blk, :, :, :, pos(b, k)], u1.at[blk, side], along_b(k))

    def step3(blk):
        recv(blk, 2, u1.at[blk, 0])
        recv(blk, 3, u1.at[blk, 1])
        for p in range(2):
            @pl.loop(0, 8)
            def _(r):
                i, j = r // 4, lax.rem(r, 4)
                total = part[blk, p, i, j, b].astype(f32) + u1[blk, 0, p, i, j].astype(f32) + u1[blk, 1, p, i, j].astype(f32)
                mid[blk, p, i, j] = total.astype(bf16)
        for k in (2, 1, 3):
            send(blk, 3 + k, mid.at[blk, :, :, pos(a, k)], u2.at[blk, k - 1], along_a(k))

    def step4(blk):
        for k in (1, 3, 2):
            recv(blk, 3 + k, u2.at[blk, k - 1])
        for p in range(2):
            for i in range(2):
                total = mid[blk, p, i, a].astype(f32)
                for k in range(3):
                    total = total + u2[blk, k, p, i].astype(f32)
                end[blk, p, i] = total.astype(bf16)
        for k in (2, 1, 3):
            d = pos(here, k)
            send(blk, 6 + k, end.at[blk, d // 2, lax.rem(d, 2)], v3.at[blk, k - 1], along_x(k))

    def step5(blk):
        for k in (1, 3, 2):
            recv(blk, 6 + k, v3.at[blk, k - 1])
        fin[blk] = end[blk, h, low].astype(f32) + v3[blk, 0].astype(f32) + v3[blk, 1].astype(f32) + v3[blk, 2].astype(f32)
        send(blk, 10, fin.at[blk, pl.ds(pl.multiple_of((1 - core) * 24, 8), 24)], swap.at[blk], mate)

    def step6(blk):
        mg[blk, :, lanes(core * 384, 384)] = fin[blk, pl.ds(pl.multiple_of(core * 24, 8), 24), :]
        recv(blk, 10, swap.at[blk])
        mg[blk, :, lanes((1 - core) * 384, 384)] = swap[blk]

    def give_sent(blk):
        remote(give, got.at[blk], ss.at[blk, 11], sr.at[blk, 11], mate).wait_send()

    def send_out(t, q):
        src, halo, dst = ((xv, XH, xo), (ev, EH, eo))[t]
        for c in range(2):
            start(remote(src.at[q, halo : halo + BINS, c * HALF : (c + 1) * HALF], dst.at[2 * h + q], rs.at[t, q, c], rr.at[t, q, h], (g, c)))

    def crossed(blk):
        remote(mv.at[blk, 1 - h, 0 : 16 * ROWS], mv.at[blk, 1 - h, 0 : 16 * ROWS], ms.at[blk, 7], mr.at[blk, 7], mate).wait_recv()

    for blk in range(3):
        hop(blk).wait_recv()
        spread(blk, 0, piece, 1, along_b)
    spread_wait(0, 0, 1, along_b)
    spread(0, 1, core * 16 + a * 4, 4, along_a)
    spread_wait(1, 0, 1, along_b)
    spread_wait(2, 0, 1, along_b)
    wait_in(0, 0)
    send_in(0, 1)
    klocal.wait()
    remote(k_ref, kv.at[1 - h], ks.at[0], ks.at[1], (g, 1 - h)).wait_recv()
    spread_wait(0, 1, 4, along_a)
    start(across(0))
    spread(1, 1, core * 16 + a * 4, 4, along_a)
    wait_edges(0, 0)
    forward(0, 0)
    own_mix.wait()
    crossed(0)
    edges_sent(0, 0)
    mix(0, 0)
    forward(1, 0)
    spread_wait(1, 1, 4, along_a)
    start(across(1))
    spread(2, 1, core * 16 + a * 4, 4, along_a)
    wait_in(0, 1)
    send_in(1, 0)
    crossed(1)
    mix(1, 0)
    forward(2, 0)
    wait_edges(0, 1)
    forward(0, 1)
    edges_sent(0, 1)
    mix(0, 1)
    spread_wait(2, 1, 4, along_a)
    start(across(2))
    forward(1, 1)
    wait_in(1, 0)
    send_in(1, 1)
    mix(1, 1)
    crossed(2)
    mix(2, 0)
    forward(2, 1)
    mix(2, 1)

    wait_edges(1, 0)
    back(2, 0)
    wait_in(1, 1)
    send_out(0, 0)
    send_out(0, 1)
    grads_give(2)
    wait_edges(1, 1)
    back(2, 1)
    grads_own(2)
    edges_sent(1, 0)
    lower(2, 0)
    edges_sent(1, 1)
    lower(2, 1)
    give_sent(2)
    grads_give(1)
    step2(2)
    back(1, 0)
    grads_own(1)
    back(1, 1)
    lower(1, 0)
    lower(1, 1)
    give_sent(1)
    grads_give(0)
    step3(2)
    back(0, 0)
    step2(1)
    grads_own(0)
    lower(0, 0)
    send_out(1, 0)
    back(0, 1)
    lower(0, 1)
    step4(2)
    send_out(1, 1)
    step3(1)
    step2(0)
    step5(2)
    step4(1)
    step6(2)
    step5(1)
    step3(0)
    step6(1)
    step4(0)
    step5(0)
    step6(0)
    give_sent(0)

    for t, dst in enumerate((xo, eo)):
        for q in range(2):
            for c in range(2):
                remote(xv.at[q, 0:BINS, 0:HALF], dst.at[2 * c + q], rs.at[t, q, 0], rr.at[t, q, c], (g, 0)).wait_recv()
    for cond, copy in pending:
        if cond is None:
            copy.wait_send()
        else:
            pl.when(cond)(copy.wait_send)


def on_device(inputs, kernels, mixers, cotangent):
    D = pltpu.SemaphoreType.DMA
    V = pltpu.VMEM
    return pl.pallas_call(
        body,
        out_shape=(
            jax.ShapeDtypeStruct((4, BINS, HALF), bf16),
            jax.ShapeDtypeStruct((4, BINS, HALF), bf16),
            jax.ShapeDtypeStruct((3, 24, HALF), f32),
        ),
        in_specs=[ANY] * 4,
        out_specs=(ANY, ANY, pl.BlockSpec(memory_space=pltpu.VMEM)),
        scratch_shapes=[
            V((2, XN, FULL), bf16), V((2, EN, FULL), bf16), V((3, 2, XN, FULL), bf16), V((3, 2, EN, FULL), bf16), V((2, EN, FULL), bf16),
            V((3, 2, FULL, HALF), bf16), V((2, 3, 3, HALF), f32),
            V((2, 2, 4, 4, ROWS, 384), bf16), V((3, 2, 2, 4, 4, ROWS, 384), bf16), V((3, 2, 2, 4, 4, ROWS, 384), bf16),
            V((3, 2, 2, 4, ROWS, 384), bf16), V((3, 2, 2, 2, 4, ROWS, 384), bf16), V((3, 2, 2, 4, ROWS, 384), bf16),
            V((3, 3, 2, 2, ROWS, 384), bf16), V((3, 2, 2, ROWS, 384), bf16),
            V((3, 3, ROWS, 384), bf16), V((3, ROWS, 384), f32), V((3, 24, 384), f32),
            D((2, 2, 2)), D((2, 2, 2)), D((2, 2, 2)), D((2, 2, 2)), D((3, 8)), D((3, 8)), D((2,)), D((2, 2, 2)), D((2, 2, 2)), D((3, 13)), D((3, 13)), D((2,)),
        ],
        compiler_params=pltpu.CompilerParams(collective_id=0, has_side_effects=True, vmem_limit_bytes=60 << 20),
    )(inputs, cotangent, mixers, kernels)


def solution(mesh):
    return jax.shard_map(
        on_device,
        mesh=mesh,
        in_specs=(P(None, "seq", "ch"), P(None, None, "ch"), P(None, None, "ch"), P(None, "seq", "ch")),
        out_specs=(P(None, "seq", "ch"), P(None, "seq", "ch"), P(None, "seq", "ch")),
        check_vma=False,
    )
```

```python
import jax
import jax.numpy as jnp
from jax import lax
from jax.experimental import pallas as pl
from jax.experimental.pallas import tpu as pltpu
from jax.sharding import PartitionSpec as P

dilations = (2, 4, 8)
MESH = pl.DeviceIdType.MESH
ANY = pl.BlockSpec(memory_space=pl.ANY)
bf16, f32 = jnp.bfloat16, jnp.float32
XH, EH = 32, 16
BINS, HALF, FULL = 256, 768, 1536
XN, EN = BINS + 2 * XH, BINS + 2 * EH
ROWS = 48
TILE = 128


def place():
    s = lax.axis_index("seq")
    h = lax.axis_index("ch")
    core = lax.rem(s, 2)
    y = lax.rem(s // 2, 4)
    z = lax.rem(s // 8, 4)
    return s, h, s // 32, z, y, core


def other(s):
    return lax.rem(s + 32, 64)


def line(core, low, a, b):
    z = a + core * (b - a)
    y = b + core * (a - b)
    return low * 32 + z * 8 + y * 2 + core


def remote(src, dst, send, recv, to):
    return pltpu.make_async_remote_copy(
        src_ref=src, dst_ref=dst, send_sem=send, recv_sem=recv, device_id=to, device_id_type=MESH
    )


def lanes(start, size, step=128):
    return pl.ds(pl.multiple_of(start, step), size)


def body(
    x_ref, e_ref, m_ref, k_ref, xo, eo, mg,
    xv, ev, acts, slopes, down, mv, kv, give, got, part, t1, u1, mid, u2, end, v3, fin, swap,
    xs, xr, es, er, ms, mr, ks, rs, rr, ss, sr, ls,
):
    s, h, low, z, y, core = place()
    g = other(s)
    a = z + core * (y - z)
    b = y + core * (z - y)
    mate = (s + 1 - 2 * core, h)
    here = 2 * h + low
    piece = core * 16 + a * 4 + b
    pending = []

    def start(copy, cond=None):
        pending.append((cond, copy))
        if cond is None:
            copy.start()
        else:
            pl.when(cond)(copy.start)
        return copy

    along_a = lambda k: (line(core, low, lax.rem(a + k, 4), b), h)
    along_b = lambda k: (line(core, low, a, lax.rem(b + k, 4)), h)

    def along_x(k):
        d = lax.rem(here + k, 4)
        return (lax.rem(d, 2) * 32 + z * 8 + y * 2 + core, d // 2)

    barrier = pltpu.get_barrier_semaphore()
    peers = [(g, 0), (g, 1), (s, 1 - h), mate]
    peers += [(other(lax.rem(g + d, 64)), h) for d in (1, 63)]
    peers += [line_of(k) for line_of in (along_a, along_b) for k in (1, 2, 3)]
    for peer in peers:
        pl.semaphore_signal(barrier, inc=1, device_id=peer, device_id_type=MESH)
    pl.semaphore_wait(barrier, len(peers))

    def rows(first, count):
        return pl.ds(pl.multiple_of(first * ROWS, ROWS), count * ROWS)

    def hop(blk):
        return remote(m_ref.at[blk, rows(piece, 1), :], mv.at[blk, h, rows(piece, 1)], ms.at[blk, 0], mr.at[blk, 0], (g, 1 - h))

    sides = ((x_ref, xv, XH), (e_ref, ev, EH))

    def send_in(t, q):
        src, dst, halo = sides[t]
        for p in range(2):
            start(remote(src.at[2 * p + q], dst.at[q, halo : halo + BINS, lanes(h * HALF, HALF)], xs.at[t, q, p], xr.at[t, q, h], (g, p)))

    def wait_in(t, q):
        src, dst, halo = sides[t]
        for c in range(2):
            remote(src.at[0], dst.at[q, halo : halo + BINS, c * HALF : (c + 1) * HALF], xs.at[t, q, 0], xr.at[t, q, c], (g, 0)).wait_recv()
        for cond, copy in edges(t, q):
            pl.when(cond)(copy.start)

    def edges(t, q):
        src, dst, halo = sides[t]
        up, down_to = (other(lax.rem(g + 1, 64)), h), (other(lax.rem(g + 63, 64)), h)
        return (
            (g < 63, remote(dst.at[q, BINS : BINS + halo], dst.at[q, 0:halo], es.at[t, q, 0], er.at[t, q, 0], up)),
            (g > 0, remote(dst.at[q, halo : 2 * halo], dst.at[q, halo + BINS : 2 * halo + BINS], es.at[t, q, 1], er.at[t, q, 1], down_to)),
        )

    def edges_sent(t, q):
        for cond, copy in edges(t, q):
            pl.when(cond)(copy.wait_send)

    def wait_edges(t, q):
        src, dst, halo = sides[t]
        pl.when(g > 0)(remote(dst.at[q, 0:halo], dst.at[q, 0:halo], es.at[t, q, 0], er.at[t, q, 0], mate).wait_recv)
        pl.when(g < 63)(remote(dst.at[q, 0:halo], dst.at[q, halo + BINS : 2 * halo + BINS], es.at[t, q, 1], er.at[t, q, 1], mate).wait_recv)

    def spread(blk, step, first, count, peer):
        for k in (1, 3, 2):
            at = (blk, step * 3 + k)
            start(remote(mv.at[blk, 1 - h, rows(first, count)], mv.at[blk, 1 - h, rows(first, count)], ms.at[*at], mr.at[*at], peer(k)))

    def spread_wait(blk, step, count, peer):
        for k in (1, 3, 2):
            at = (blk, step * 3 + k)
            remote(mv.at[blk, 1 - h, 0 : count * ROWS], mv.at[blk, 1 - h, 0 : count * ROWS], ms.at[*at], mr.at[*at], peer(k)).wait_recv()

    def across(blk):
        at = mv.at[blk, 1 - h, rows(core * 16, 16)]
        return remote(at, at, ms.at[blk, 7], mr.at[blk, 7], mate)

    for blk in range(3):
        start(hop(blk))
    send_in(0, 0)
    kcopy = start(remote(k_ref, kv.at[h], ks.at[0], ks.at[1], (g, 1 - h)))
    klocal = pltpu.make_async_copy(k_ref, kv.at[h], ls.at[1])
    klocal.start()
    own_mix = pltpu.make_async_copy(m_ref, mv.at[:, h], ls.at[0])
    own_mix.start()

    def zero_edges(ref, q, halo):
        pl.when(g == 0)(lambda: put_zero(ref, q, 0, halo))
        pl.when(g == 63)(lambda: put_zero(ref, q, BINS + halo, halo))

    def put_zero(ref, q, first, count):
        ref[q, first : first + count, :] = jnp.zeros((count, FULL), bf16)

    for q in range(2):
        zero_edges(xv, q, XH)
        zero_edges(ev, q, EH)

    def weight(blk, tap, part_of, at):
        return kv[part_of, blk, tap : tap + 1, lanes(at * TILE, TILE)]

    def column_tiles(fn):
        for part_of in range(2):
            @pl.loop(0, HALF // TILE)
            def _(j):
                fn(part_of, j, lanes(part_of * HALF + j * TILE, TILE))

    def forward(blk, q):
        d = dilations[blk]

        def tile(part_of, j, cols):
            value = xv[q, :, cols].astype(f32)
            pre = (
                weight(blk, 0, part_of, j) * pltpu.roll(value, d, 0)
                + weight(blk, 1, part_of, j) * value
                + weight(blk, 2, part_of, j) * pltpu.roll(value, XN - d, 0)
            )
            half = 0.5 * (1.0 + lax.erf(pre * 0.7071067811865476))
            acts[blk, q, :, cols] = (pre * half).astype(bf16)
            slope = half + pre * jnp.exp(-0.5 * pre * pre) * 0.3989422804014327
            slopes[blk, q, :, cols] = slope[XH - EH : XH + BINS + EH].astype(bf16)

        column_tiles(tile)

    def mix(blk, q):
        span = pl.ds(0, XN) if blk < 2 else pl.ds(XH, BINS)
        @pl.loop(0, 2)
        def _(part_of):
            cols = lanes(part_of * HALF, HALF)
            mixed = jnp.dot(acts[blk, q, span, :], mv[blk, part_of], preferred_element_type=f32)
            xv[q, span, cols] = (xv[q, span, cols].astype(f32) + mixed).astype(bf16)

        if blk < 2:
            zero_edges(xv, q, XH)

    def back(blk, q):
        total = None
        for part_of in range(2):
            term = lax.dot_general(
                ev[q, :, part_of * HALF : (part_of + 1) * HALF], mv[blk, part_of],
                (((1,), (1,)), ((), ())), preferred_element_type=f32)
            total = term if total is None else total + term
        down[q] = (total * slopes[blk, q].astype(f32)).astype(bf16)
        zero_edges(down, q, EH)

    def lower(blk, q):
        d = dilations[blk]

        def tile(part_of, j, cols):
            value = down[q, :, cols].astype(f32)
            total = (
                ev[q, :, cols].astype(f32)
                + weight(blk, 0, part_of, j) * pltpu.roll(value, EN - d, 0)
                + weight(blk, 1, part_of, j) * value
                + weight(blk, 2, part_of, j) * pltpu.roll(value, d, 0)
            )
            ev[q, :, cols] = total.astype(bf16)

        column_tiles(tile)

    def product(blk, of, c):
        total = None
        for q in range(2):
            right = jnp.concatenate([ev[q, EH : EH + BINS, lanes(p * HALF + of * 384, 384)] for p in range(2)], axis=1)
            term = lax.dot_general(
                acts[blk, q, XH : XH + BINS, lanes(c * HALF, HALF)], right,
                (((0,), (0,)), ((), ())), preferred_element_type=f32)
            total = term if total is None else total + term
        return total * (1.0 / 256.0)

    def spot(of, r):
        zz, yy = r // 4, r % 4
        return zz + of * (yy - zz), yy + of * (zz - yy)

    def given(blk, c):
        return remote(give.at[:, c], got.at[blk, :, c], ss.at[blk, 18 + c], sr.at[blk, 18 + c], mate)

    def grads_give(blk):
        for c in range(2):
            total = product(blk, 1 - core, c).astype(bf16)
            for p in range(2):
                for r in range(16):
                    give[(p, c, *spot(1 - core, r))] = total[r * ROWS : (r + 1) * ROWS, p * 384 : (p + 1) * 384]
            given(blk, c).start()

    def grads_own(blk):
        for c in range(2):
            given(blk, c).wait_recv()
            total = product(blk, core, c)
            for p in range(2):
                for r in range(16):
                    at = (blk, p, c, *spot(core, r))
                    part[at] = (total[r * ROWS : (r + 1) * ROWS, p * 384 : (p + 1) * 384] + got[at].astype(f32)).astype(bf16)
            for p in range(2):
                send(blk, 2 * p + c, part.at[blk, p, c, :, pos(b, 2)], t1.at[blk, p, c], along_b(1 + 2 * p))

    def add(dst, src):
        dst[...] = (dst[...].astype(f32) + src[...].astype(f32)).astype(bf16)

    def send(blk, n, src, dst, to):
        return start(remote(src, dst, ss.at[blk, n], sr.at[blk, n], to))

    def recv(blk, n, dst):
        remote(dst, dst, ss.at[blk, n], sr.at[blk, n], mate).wait_recv()

    pos = lambda here_, k: lax.rem(here_ + k, 4)

    def step2(blk):
        for c in range(2):
            for side, k in ((0, 1), (1, 3)):
                recv(blk, 2 * side + c, t1.at[blk, side, c])

                @pl.loop(0, 4)
                def _(r):
                    add(part.at[blk, side, c, r, pos(b, k)], t1.at[blk, side, c, r])

                send(blk, 4 + 2 * side + c, part.at[blk, :, c, :, pos(b, k)], u1.at[blk, side, :, c], along_b(k))

    def step3(blk):
        for c in range(2):
            recv(blk, 4 + c, u1.at[blk, 0, :, c])
            recv(blk, 6 + c, u1.at[blk, 1, :, c])
            for p in range(2):
                @pl.loop(0, 4)
                def _(j):
                    total = part[blk, p, c, j, b].astype(f32) + u1[blk, 0, p, c, j].astype(f32) + u1[blk, 1, p, c, j].astype(f32)
                    mid[blk, p, c, j] = total.astype(bf16)
            for k in (2, 1, 3):
                send(blk, 6 + 2 * k + c, mid.at[blk, :, c, pos(a, k)], u2.at[blk, k - 1, :, c], along_a(k))

    def step4(blk):
        for k in (1, 3, 2):
            for c in range(2):
                recv(blk, 6 + 2 * k + c, u2.at[blk, k - 1, :, c])
        for p in range(2):
            for i in range(2):
                total = mid[blk, p, i, a].astype(f32)
                for k in range(3):
                    total = total + u2[blk, k, p, i].astype(f32)
                end[blk, p, i] = total.astype(bf16)
        for k in (2, 1, 3):
            d = pos(here, k)
            send(blk, 13 + k, end.at[blk, d // 2, lax.rem(d, 2)], v3.at[blk, k - 1], along_x(k))

    def step5(blk):
        for k in (1, 3, 2):
            recv(blk, 13 + k, v3.at[blk, k - 1])
        fin[blk] = end[blk, h, low].astype(f32) + v3[blk, 0].astype(f32) + v3[blk, 1].astype(f32) + v3[blk, 2].astype(f32)
        send(blk, 17, fin.at[blk, pl.ds(pl.multiple_of((1 - core) * 24, 8), 24)], swap.at[blk], mate)

    def step6(blk):
        mg[blk, :, lanes(core * 384, 384)] = fin[blk, pl.ds(pl.multiple_of(core * 24, 8), 24), :]
        recv(blk, 17, swap.at[blk])
        mg[blk, :, lanes((1 - core) * 384, 384)] = swap[blk]

    def give_sent(blk):
        for c in range(2):
            given(blk, c).wait_send()

    def send_out(t, q):
        src, halo, dst = ((xv, XH, xo), (ev, EH, eo))[t]
        for c in range(2):
            start(remote(src.at[q, halo : halo + BINS, c * HALF : (c + 1) * HALF], dst.at[2 * h + q], rs.at[t, q, c], rr.at[t, q, h], (g, c)))

    def crossed(blk):
        remote(mv.at[blk, 1 - h, 0 : 16 * ROWS], mv.at[blk, 1 - h, 0 : 16 * ROWS], ms.at[blk, 7], mr.at[blk, 7], mate).wait_recv()

    for blk in range(3):
        hop(blk).wait_recv()
        spread(blk, 0, piece, 1, along_b)
    spread_wait(0, 0, 1, along_b)
    spread(0, 1, core * 16 + a * 4, 4, along_a)
    spread_wait(1, 0, 1, along_b)
    spread_wait(2, 0, 1, along_b)
    wait_in(0, 0)
    send_in(0, 1)
    klocal.wait()
    remote(k_ref, kv.at[1 - h], ks.at[0], ks.at[1], (g, 1 - h)).wait_recv()
    spread_wait(0, 1, 4, along_a)
    start(across(0))
    spread(1, 1, core * 16 + a * 4, 4, along_a)
    wait_edges(0, 0)
    forward(0, 0)
    own_mix.wait()
    crossed(0)
    edges_sent(0, 0)
    mix(0, 0)
    forward(1, 0)
    spread_wait(1, 1, 4, along_a)
    start(across(1))
    spread(2, 1, core * 16 + a * 4, 4, along_a)
    wait_in(0, 1)
    send_in(1, 0)
    crossed(1)
    mix(1, 0)
    forward(2, 0)
    wait_edges(0, 1)
    forward(0, 1)
    edges_sent(0, 1)
    mix(0, 1)
    spread_wait(2, 1, 4, along_a)
    start(across(2))
    forward(1, 1)
    wait_in(1, 0)
    send_in(1, 1)
    mix(1, 1)
    crossed(2)
    mix(2, 0)
    forward(2, 1)
    mix(2, 1)

    wait_edges(1, 0)
    back(2, 0)
    wait_in(1, 1)
    send_out(0, 0)
    send_out(0, 1)
    grads_give(2)
    wait_edges(1, 1)
    back(2, 1)
    grads_own(2)
    edges_sent(1, 0)
    lower(2, 0)
    edges_sent(1, 1)
    lower(2, 1)
    give_sent(2)
    grads_give(1)
    step2(2)
    back(1, 0)
    grads_own(1)
    back(1, 1)
    lower(1, 0)
    lower(1, 1)
    give_sent(1)
    grads_give(0)
    back(0, 0)
    grads_own(0)
    step2(1)
    step3(2)
    lower(0, 0)
    send_out(1, 0)
    back(0, 1)
    lower(0, 1)
    send_out(1, 1)
    step2(0)
    step4(2)
    step3(1)
    step5(2)
    step4(1)
    step6(2)
    step3(0)
    step5(1)
    step6(1)
    step4(0)
    step5(0)
    step6(0)
    give_sent(0)

    for t, dst in enumerate((xo, eo)):
        for q in range(2):
            for c in range(2):
                remote(xv.at[q, 0:BINS, 0:HALF], dst.at[2 * c + q], rs.at[t, q, 0], rr.at[t, q, c], (g, 0)).wait_recv()
    for cond, copy in pending:
        if cond is None:
            copy.wait_send()
        else:
            pl.when(cond)(copy.wait_send)


def on_device(inputs, kernels, mixers, cotangent):
    D = pltpu.SemaphoreType.DMA
    V = pltpu.VMEM
    return pl.pallas_call(
        body,
        out_shape=(
            jax.ShapeDtypeStruct((4, BINS, HALF), bf16),
            jax.ShapeDtypeStruct((4, BINS, HALF), bf16),
            jax.ShapeDtypeStruct((3, 24, HALF), f32),
        ),
        in_specs=[ANY] * 4,
        out_specs=(ANY, ANY, pl.BlockSpec(memory_space=pltpu.VMEM)),
        scratch_shapes=[
            V((2, XN, FULL), bf16), V((2, EN, FULL), bf16), V((3, 2, XN, FULL), bf16), V((3, 2, EN, FULL), bf16), V((2, EN, FULL), bf16),
            V((3, 2, FULL, HALF), bf16), V((2, 3, 3, HALF), f32),
            V((2, 2, 4, 4, ROWS, 384), bf16), V((3, 2, 2, 4, 4, ROWS, 384), bf16), V((3, 2, 2, 4, 4, ROWS, 384), bf16),
            V((3, 2, 2, 4, ROWS, 384), bf16), V((3, 2, 2, 2, 4, ROWS, 384), bf16), V((3, 2, 2, 4, ROWS, 384), bf16),
            V((3, 3, 2, 2, ROWS, 384), bf16), V((3, 2, 2, ROWS, 384), bf16),
            V((3, 3, ROWS, 384), bf16), V((3, ROWS, 384), f32), V((3, 24, 384), f32),
            D((2, 2, 2)), D((2, 2, 2)), D((2, 2, 2)), D((2, 2, 2)), D((3, 8)), D((3, 8)), D((2,)), D((2, 2, 2)), D((2, 2, 2)), D((3, 20)), D((3, 20)), D((2,)),
        ],
        compiler_params=pltpu.CompilerParams(collective_id=0, has_side_effects=True, vmem_limit_bytes=60 << 20),
    )(inputs, cotangent, mixers, kernels)


def solution(mesh):
    return jax.shard_map(
        on_device,
        mesh=mesh,
        in_specs=(P(None, "seq", "ch"), P(None, None, "ch"), P(None, None, "ch"), P(None, "seq", "ch")),
        out_specs=(P(None, "seq", "ch"), P(None, "seq", "ch"), P(None, "seq", "ch")),
        check_vma=False,
    )
```

```python
import jax
import jax.numpy as jnp
from jax import lax
from jax.experimental import pallas as pl
from jax.experimental.pallas import tpu as pltpu
from jax.sharding import PartitionSpec as P

dilations = (2, 4, 8)
MESH = pl.DeviceIdType.MESH
ANY = pl.BlockSpec(memory_space=pl.ANY)
bf16, f32 = jnp.bfloat16, jnp.float32
XH, EH = 32, 16
BINS, HALF, FULL = 256, 768, 1536
XN, EN = BINS + 2 * XH, BINS + 2 * EH
ROWS = 48
TILE = 128


def place():
    s = lax.axis_index("seq")
    h = lax.axis_index("ch")
    core = lax.rem(s, 2)
    y = lax.rem(s // 2, 4)
    z = lax.rem(s // 8, 4)
    return s, h, s // 32, z, y, core


def other(s):
    return lax.rem(s + 32, 64)


def line(core, low, a, b):
    z = a + core * (b - a)
    y = b + core * (a - b)
    return low * 32 + z * 8 + y * 2 + core


def remote(src, dst, send, recv, to):
    return pltpu.make_async_remote_copy(
        src_ref=src, dst_ref=dst, send_sem=send, recv_sem=recv, device_id=to, device_id_type=MESH
    )


def lanes(start, size, step=128):
    return pl.ds(pl.multiple_of(start, step), size)


def body(
    x_ref, e_ref, m_ref, k_ref, xo, eo, mg,
    xv, ev, acts, slopes, down, mv, kv, give, got, part, t1, u1, mid, u2, end, v3, fin, swap,
    xs, xr, es, er, ms, mr, ks, rs, rr, ss, sr, ls,
):
    s, h, low, z, y, core = place()
    g = other(s)
    a = z + core * (y - z)
    b = y + core * (z - y)
    mate = (s + 1 - 2 * core, h)
    here = 2 * h + low
    piece = core * 16 + a * 4 + b
    pending = []

    def start(copy, cond=None):
        pending.append((cond, copy))
        if cond is None:
            copy.start()
        else:
            pl.when(cond)(copy.start)
        return copy

    along_a = lambda k: (line(core, low, lax.rem(a + k, 4), b), h)
    along_b = lambda k: (line(core, low, a, lax.rem(b + k, 4)), h)

    def along_x(k):
        d = lax.rem(here + k, 4)
        return (lax.rem(d, 2) * 32 + z * 8 + y * 2 + core, d // 2)

    barrier = pltpu.get_barrier_semaphore()
    peers = [(g, 0), (g, 1), (s, 1 - h), mate]
    peers += [(other(lax.rem(g + d, 64)), h) for d in (1, 63)]
    peers += [line_of(k) for line_of in (along_a, along_b) for k in (1, 2, 3)]
    for peer in peers:
        pl.semaphore_signal(barrier, inc=1, device_id=peer, device_id_type=MESH)
    pl.semaphore_wait(barrier, len(peers))

    def rows(first, count):
        return pl.ds(pl.multiple_of(first * ROWS, ROWS), count * ROWS)

    def hop(blk):
        return remote(m_ref.at[blk, rows(piece, 1), :], mv.at[blk, h, rows(piece, 1)], ms.at[blk, 0], mr.at[blk, 0], (g, 1 - h))

    sides = ((x_ref, xv, XH), (e_ref, ev, EH))

    def send_in(t, q):
        src, dst, halo = sides[t]
        for p in range(2):
            start(remote(src.at[2 * p + q], dst.at[q, halo : halo + BINS, lanes(h * HALF, HALF)], xs.at[t, q, p], xr.at[t, q, h], (g, p)))

    def wait_in(t, q):
        src, dst, halo = sides[t]
        for c in range(2):
            remote(src.at[0], dst.at[q, halo : halo + BINS, c * HALF : (c + 1) * HALF], xs.at[t, q, 0], xr.at[t, q, c], (g, 0)).wait_recv()
        for cond, copy in edges(t, q):
            pl.when(cond)(copy.start)

    def edges(t, q):
        src, dst, halo = sides[t]
        up, down_to = (other(lax.rem(g + 1, 64)), h), (other(lax.rem(g + 63, 64)), h)
        return (
            (g < 63, remote(dst.at[q, BINS : BINS + halo], dst.at[q, 0:halo], es.at[t, q, 0], er.at[t, q, 0], up)),
            (g > 0, remote(dst.at[q, halo : 2 * halo], dst.at[q, halo + BINS : 2 * halo + BINS], es.at[t, q, 1], er.at[t, q, 1], down_to)),
        )

    def edges_sent(t, q):
        for cond, copy in edges(t, q):
            pl.when(cond)(copy.wait_send)

    def wait_edges(t, q):
        src, dst, halo = sides[t]
        pl.when(g > 0)(remote(dst.at[q, 0:halo], dst.at[q, 0:halo], es.at[t, q, 0], er.at[t, q, 0], mate).wait_recv)
        pl.when(g < 63)(remote(dst.at[q, 0:halo], dst.at[q, halo + BINS : 2 * halo + BINS], es.at[t, q, 1], er.at[t, q, 1], mate).wait_recv)

    def spread(blk, step, first, count, peer):
        for k in (1, 3, 2):
            at = (blk, step * 3 + k)
            start(remote(mv.at[blk, 1 - h, rows(first, count)], mv.at[blk, 1 - h, rows(first, count)], ms.at[*at], mr.at[*at], peer(k)))

    def spread_wait(blk, step, count, peer):
        for k in (1, 3, 2):
            at = (blk, step * 3 + k)
            remote(mv.at[blk, 1 - h, 0 : count * ROWS], mv.at[blk, 1 - h, 0 : count * ROWS], ms.at[*at], mr.at[*at], peer(k)).wait_recv()

    def across(blk):
        at = mv.at[blk, 1 - h, rows(core * 16, 16)]
        return remote(at, at, ms.at[blk, 7], mr.at[blk, 7], mate)

    for blk in range(3):
        start(hop(blk))
    send_in(0, 0)
    kcopy = start(remote(k_ref, kv.at[h], ks.at[0], ks.at[1], (g, 1 - h)))
    klocal = pltpu.make_async_copy(k_ref, kv.at[h], ls.at[1])
    klocal.start()
    own_mix = pltpu.make_async_copy(m_ref, mv.at[:, h], ls.at[0])
    own_mix.start()

    def zero_edges(ref, q, halo):
        pl.when(g == 0)(lambda: put_zero(ref, q, 0, halo))
        pl.when(g == 63)(lambda: put_zero(ref, q, BINS + halo, halo))

    def put_zero(ref, q, first, count):
        ref[q, first : first + count, :] = jnp.zeros((count, FULL), bf16)

    for q in range(2):
        zero_edges(xv, q, XH)
        zero_edges(ev, q, EH)

    def weight(blk, tap, part_of, at):
        return kv[part_of, blk, tap : tap + 1, lanes(at * TILE, TILE)]

    def column_tiles(fn):
        for part_of in range(2):
            @pl.loop(0, HALF // TILE)
            def _(j):
                fn(part_of, j, lanes(part_of * HALF + j * TILE, TILE))

    def forward(blk, q):
        d = dilations[blk]

        def tile(part_of, j, cols):
            value = xv[q, :, cols].astype(f32)
            pre = (
                weight(blk, 0, part_of, j) * pltpu.roll(value, d, 0)
                + weight(blk, 1, part_of, j) * value
                + weight(blk, 2, part_of, j) * pltpu.roll(value, XN - d, 0)
            )
            half = 0.5 * (1.0 + lax.erf(pre * 0.7071067811865476))
            acts[blk, q, :, cols] = (pre * half).astype(bf16)
            slope = half + pre * jnp.exp(-0.5 * pre * pre) * 0.3989422804014327
            slopes[blk, q, :, cols] = slope[XH - EH : XH + BINS + EH].astype(bf16)

        column_tiles(tile)

    def mix(blk, q):
        span = pl.ds(0, XN) if blk < 2 else pl.ds(XH, BINS)
        @pl.loop(0, 2)
        def _(part_of):
            cols = lanes(part_of * HALF, HALF)
            mixed = jnp.dot(acts[blk, q, span, :], mv[blk, part_of], preferred_element_type=f32)
            xv[q, span, cols] = (xv[q, span, cols].astype(f32) + mixed).astype(bf16)

        if blk < 2:
            zero_edges(xv, q, XH)

    def back(blk, q):
        total = None
        for part_of in range(2):
            term = lax.dot_general(
                ev[q, :, part_of * HALF : (part_of + 1) * HALF], mv[blk, part_of],
                (((1,), (1,)), ((), ())), preferred_element_type=f32)
            total = term if total is None else total + term
        down[q] = (total * slopes[blk, q].astype(f32)).astype(bf16)
        zero_edges(down, q, EH)

    def lower(blk, q):
        d = dilations[blk]

        def tile(part_of, j, cols):
            value = down[q, :, cols].astype(f32)
            total = (
                ev[q, :, cols].astype(f32)
                + weight(blk, 0, part_of, j) * pltpu.roll(value, EN - d, 0)
                + weight(blk, 1, part_of, j) * value
                + weight(blk, 2, part_of, j) * pltpu.roll(value, d, 0)
            )
            ev[q, :, cols] = total.astype(bf16)

        column_tiles(tile)

    def product(blk, of, c):
        total = None
        for q in range(2):
            right = jnp.concatenate([ev[q, EH : EH + BINS, lanes(p * HALF + of * 384, 384)] for p in range(2)], axis=1)
            term = lax.dot_general(
                acts[blk, q, XH : XH + BINS, lanes(c * HALF, HALF)], right,
                (((0,), (0,)), ((), ())), preferred_element_type=f32)
            total = term if total is None else total + term
        return total * (1.0 / 256.0)

    def spot(of, r):
        zz, yy = r // 4, r % 4
        return zz + of * (yy - zz), yy + of * (zz - yy)

    def given(blk, c):
        return remote(give.at[:, c], got.at[blk, :, c], ss.at[blk, 18 + c], sr.at[blk, 18 + c], mate)

    def grads_give(blk):
        for c in range(2):
            total = product(blk, 1 - core, c).astype(bf16)
            for p in range(2):
                for r in range(16):
                    give[(p, c, *spot(1 - core, r))] = total[r * ROWS : (r + 1) * ROWS, p * 384 : (p + 1) * 384]
            given(blk, c).start()

    def grads_own(blk):
        for c in range(2):
            given(blk, c).wait_recv()
            total = product(blk, core, c)
            for p in range(2):
                for r in range(16):
                    at = (blk, p, c, *spot(core, r))
                    part[at] = (total[r * ROWS : (r + 1) * ROWS, p * 384 : (p + 1) * 384] + got[at].astype(f32)).astype(bf16)
            for p in range(2):
                send(blk, 2 * p + c, part.at[blk, p, c, :, pos(b, 2)], t1.at[blk, p, c], along_b(1 + 2 * p))

    def add(dst, src):
        dst[...] = (dst[...].astype(f32) + src[...].astype(f32)).astype(bf16)

    def send(blk, n, src, dst, to):
        return start(remote(src, dst, ss.at[blk, n], sr.at[blk, n], to))

    def recv(blk, n, dst):
        remote(dst, dst, ss.at[blk, n], sr.at[blk, n], mate).wait_recv()

    pos = lambda here_, k: lax.rem(here_ + k, 4)

    def step2(blk):
        for c in range(2):
            for side, k in ((0, 1), (1, 3)):
                recv(blk, 2 * side + c, t1.at[blk, side, c])

                @pl.loop(0, 4)
                def _(r):
                    add(part.at[blk, side, c, r, pos(b, k)], t1.at[blk, side, c, r])

                send(blk, 4 + 2 * side + c, part.at[blk, :, c, :, pos(b, k)], u1.at[blk, side, :, c], along_b(k))

    def step3(blk):
        for c in range(2):
            recv(blk, 4 + c, u1.at[blk, 0, :, c])
            recv(blk, 6 + c, u1.at[blk, 1, :, c])
            for p in range(2):
                @pl.loop(0, 4)
                def _(j):
                    total = part[blk, p, c, j, b].astype(f32) + u1[blk, 0, p, c, j].astype(f32) + u1[blk, 1, p, c, j].astype(f32)
                    mid[blk, p, c, j] = total.astype(bf16)
            for k in (2, 1, 3):
                send(blk, 6 + 2 * k + c, mid.at[blk, :, c, pos(a, k)], u2.at[blk, k - 1, :, c], along_a(k))

    def step4(blk):
        for k in (1, 3, 2):
            for c in range(2):
                recv(blk, 6 + 2 * k + c, u2.at[blk, k - 1, :, c])
        for p in range(2):
            for i in range(2):
                total = mid[blk, p, i, a].astype(f32)
                for k in range(3):
                    total = total + u2[blk, k, p, i].astype(f32)
                end[blk, p, i] = total.astype(bf16)
        for k in (2, 1, 3):
            d = pos(here, k)
            send(blk, 13 + k, end.at[blk, d // 2, lax.rem(d, 2)], v3.at[blk, k - 1], along_x(k))

    def step5(blk):
        for k in (1, 3, 2):
            recv(blk, 13 + k, v3.at[blk, k - 1])
        fin[blk] = end[blk, h, low].astype(f32) + v3[blk, 0].astype(f32) + v3[blk, 1].astype(f32) + v3[blk, 2].astype(f32)
        send(blk, 17, fin.at[blk, pl.ds(pl.multiple_of((1 - core) * 24, 8), 24)], swap.at[blk], mate)

    def step6(blk):
        mg[blk, :, lanes(core * 384, 384)] = fin[blk, pl.ds(pl.multiple_of(core * 24, 8), 24), :]
        recv(blk, 17, swap.at[blk])
        mg[blk, :, lanes((1 - core) * 384, 384)] = swap[blk]

    def give_sent(blk):
        for c in range(2):
            given(blk, c).wait_send()

    def send_out(t, q):
        src, halo, dst = ((xv, XH, xo), (ev, EH, eo))[t]
        for c in range(2):
            start(remote(src.at[q, halo : halo + BINS, c * HALF : (c + 1) * HALF], dst.at[2 * h + q], rs.at[t, q, c], rr.at[t, q, h], (g, c)))

    def crossed(blk):
        remote(mv.at[blk, 1 - h, 0 : 16 * ROWS], mv.at[blk, 1 - h, 0 : 16 * ROWS], ms.at[blk, 7], mr.at[blk, 7], mate).wait_recv()

    for blk in range(3):
        hop(blk).wait_recv()
        spread(blk, 0, piece, 1, along_b)
    spread_wait(0, 0, 1, along_b)
    spread(0, 1, core * 16 + a * 4, 4, along_a)
    spread_wait(1, 0, 1, along_b)
    spread_wait(2, 0, 1, along_b)
    wait_in(0, 0)
    send_in(0, 1)
    klocal.wait()
    remote(k_ref, kv.at[1 - h], ks.at[0], ks.at[1], (g, 1 - h)).wait_recv()
    spread_wait(0, 1, 4, along_a)
    start(across(0))
    spread(1, 1, core * 16 + a * 4, 4, along_a)
    wait_edges(0, 0)
    forward(0, 0)
    own_mix.wait()
    crossed(0)
    edges_sent(0, 0)
    mix(0, 0)
    forward(1, 0)
    spread_wait(1, 1, 4, along_a)
    start(across(1))
    spread(2, 1, core * 16 + a * 4, 4, along_a)
    wait_in(0, 1)
    send_in(1, 0)
    crossed(1)
    mix(1, 0)
    forward(2, 0)
    wait_edges(0, 1)
    forward(0, 1)
    edges_sent(0, 1)
    mix(0, 1)
    spread_wait(2, 1, 4, along_a)
    start(across(2))
    forward(1, 1)
    wait_in(1, 0)
    send_in(1, 1)
    mix(1, 1)
    crossed(2)
    mix(2, 0)
    forward(2, 1)
    mix(2, 1)

    wait_edges(1, 0)
    back(2, 0)
    wait_in(1, 1)
    send_out(0, 0)
    send_out(0, 1)
    grads_give(2)
    wait_edges(1, 1)
    back(2, 1)
    grads_own(2)
    edges_sent(1, 0)
    lower(2, 0)
    edges_sent(1, 1)
    lower(2, 1)
    give_sent(2)
    grads_give(1)
    back(1, 0)
    grads_own(1)
    step2(2)
    back(1, 1)
    lower(1, 0)
    lower(1, 1)
    give_sent(1)
    grads_give(0)
    back(0, 0)
    grads_own(0)
    step2(1)
    step3(2)
    lower(0, 0)
    send_out(1, 0)
    back(0, 1)
    lower(0, 1)
    send_out(1, 1)
    step2(0)
    step4(2)
    step3(1)
    step5(2)
    step4(1)
    step6(2)
    step3(0)
    step5(1)
    step6(1)
    step4(0)
    step5(0)
    step6(0)
    give_sent(0)

    for t, dst in enumerate((xo, eo)):
        for q in range(2):
            for c in range(2):
                remote(xv.at[q, 0:BINS, 0:HALF], dst.at[2 * c + q], rs.at[t, q, 0], rr.at[t, q, c], (g, 0)).wait_recv()
    for cond, copy in pending:
        if cond is None:
            copy.wait_send()
        else:
            pl.when(cond)(copy.wait_send)


def on_device(inputs, kernels, mixers, cotangent):
    D = pltpu.SemaphoreType.DMA
    V = pltpu.VMEM
    return pl.pallas_call(
        body,
        out_shape=(
            jax.ShapeDtypeStruct((4, BINS, HALF), bf16),
            jax.ShapeDtypeStruct((4, BINS, HALF), bf16),
            jax.ShapeDtypeStruct((3, 24, HALF), f32),
        ),
        in_specs=[ANY] * 4,
        out_specs=(ANY, ANY, pl.BlockSpec(memory_space=pltpu.VMEM)),
        scratch_shapes=[
            V((2, XN, FULL), bf16), V((2, EN, FULL), bf16), V((3, 2, XN, FULL), bf16), V((3, 2, EN, FULL), bf16), V((2, EN, FULL), bf16),
            V((3, 2, FULL, HALF), bf16), V((2, 3, 3, HALF), f32),
            V((2, 2, 4, 4, ROWS, 384), bf16), V((3, 2, 2, 4, 4, ROWS, 384), bf16), V((3, 2, 2, 4, 4, ROWS, 384), bf16),
            V((3, 2, 2, 4, ROWS, 384), bf16), V((3, 2, 2, 2, 4, ROWS, 384), bf16), V((3, 2, 2, 4, ROWS, 384), bf16),
            V((3, 3, 2, 2, ROWS, 384), bf16), V((3, 2, 2, ROWS, 384), bf16),
            V((3, 3, ROWS, 384), bf16), V((3, ROWS, 384), f32), V((3, 24, 384), f32),
            D((2, 2, 2)), D((2, 2, 2)), D((2, 2, 2)), D((2, 2, 2)), D((3, 8)), D((3, 8)), D((2,)), D((2, 2, 2)), D((2, 2, 2)), D((3, 20)), D((3, 20)), D((2,)),
        ],
        compiler_params=pltpu.CompilerParams(collective_id=0, has_side_effects=True, vmem_limit_bytes=60 << 20),
    )(inputs, cotangent, mixers, kernels)


def solution(mesh):
    return jax.shard_map(
        on_device,
        mesh=mesh,
        in_specs=(P(None, "seq", "ch"), P(None, None, "ch"), P(None, None, "ch"), P(None, "seq", "ch")),
        out_specs=(P(None, "seq", "ch"), P(None, "seq", "ch"), P(None, "seq", "ch")),
        check_vma=False,
    )
```
